32 devices in a mesh: section: 4 (over y, x), seq: 8 (over z, core).
Axes of the slice: x: 2, y: 2, z: 4, core: 2. Of those that a mesh axis runs over, the one named last changes fastest.
Arguments:
- tokens: bfloat16 [1024, 1024], P('seq'), may hold values from -6 to 6
- cotangent: bfloat16 [1024, 1024], P('seq'), may hold values from -6 to 6
- norm_gain: float32 [4, 1024], P('section'), may hold values from 0.1 to 1.9
- w_inner: bfloat16 [4, 1024, 2048], P('section'), may hold values from -0.1875 to 0.1875
- w_outer: bfloat16 [4, 1024, 1024], P('section'), may hold values from -0.75 to 0.75
- rpe_periods: int32 [4, 32], P('section'), may hold values from 1 to 511
- rpe_in: float32 [4, 64, 64], P('section'), may hold values from -0.75 to 0.75
- rpe_mid: float32 [4, 64, 64], P('section'), may hold values from -0.75 to 0.75
- rpe_out: float32 [4, 64, 1024], P('section', None, 'seq'), may hold values from -3 to 3
- decay: float32 [4, 1024], P('section', 'seq'), may hold values from 0.00048828125 to 0.03
Outputs:
- section_out: bfloat16 [4, 1024, 1024], P('section', 'seq')
- section_in_grad: bfloat16 [4, 1024, 1024], P('section', 'seq')
- inner_grad: float32 [4, 1024, 2048], P('section', 'seq')
- outer_grad: float32 [4, 1024, 1024], P('section', 'seq')
The draws below stay inside these ranges and needn't reach their ends.
All inputs are finite; a program needn't handle non-finite values.
Results may differ from the reference program's by a relative error of at most 0.025.
Values may be sent and summed in bfloat16 or wider, within the bound.
A program may use at most 128 MiB of HBM per device.

```python
import math
import jax
import jax.numpy as jnp
from jax import lax

D = 1024
RPE = 64
FREQS = 32
SECTIONS = 4
LENGTH = 1024


def with_ends(result, rng, least, high):
    shape = result.shape
    spot = [jax.random.randint(jax.random.fold_in(rng, axis), (), 0, shape[axis]) for axis in range(len(shape))]
    result = result.at[tuple(spot)].set(least)
    longest = shape.index(max(shape))
    spot[longest] = (spot[longest] + 1) % shape[longest]
    return result.at[tuple(spot)].set(high)


def with_spikes(entries, own_key, source, target, parts, factor):
    def block_of(dim):
        return (jnp.arange(entries.shape[dim]) // (entries.shape[dim] // parts)).reshape((-1,) + (1,) * (entries.ndim - 1 - dim))

    first = jax.random.permutation(own_key, parts)[block_of(target)]
    far = (block_of(target) + parts // 2) % parts
    return jnp.where((block_of(source) == first) | (block_of(source) == far), factor * entries, entries)


def steps_of(rng, extent, split, low, high):
    level, own = 1.0, jax.random.fold_in(rng, 6)
    for dim, shards_of in split:
        draws = jnp.exp(jax.random.uniform(jax.random.fold_in(own, dim), (shards_of,), jnp.float32, low / len(split), high / len(split)))
        level = level * jnp.repeat(draws, extent[dim] // shards_of).reshape([-1 if axis == dim else 1 for axis in range(len(extent))])
    return level


def gaussian(key, extent, spread, reach, split=(), kind=jnp.bfloat16):
    array = jax.random.normal(key, extent, jnp.float32) * spread
    if len(split) > 0:
        array = steps_of(key, extent, split, -0.22, 0.18) * array
    return jnp.clip(array, min=-reach, max=reach).astype(kind)


def noise_with(key, extent, spread, bound, split, heavy, kind=jnp.bfloat16):
    entries = spread * jax.random.normal(key, extent, jnp.float32)
    if split:
        entries = entries * steps_of(key, extent, split, -0.22, 0.18)
    return jnp.clip(with_spikes(entries, jax.random.fold_in(key, 3), *heavy), -bound, bound).astype(kind)


def setup_inputs(seed: int = 0) -> dict:
    key_of = jax.random.split(jax.random.key(seed), 11)
    return {
        "tokens": noise_with(key_of[0], (LENGTH, D), 1.0, 6.0, ((0, 8),), (0, 1, 8, 2.0)),
        "cotangent": gaussian(key_of[1], (LENGTH, D), 1.0, 6.0, ((0, 8),)),
        "norm_gain": jnp.clip(1.0 + 0.18 * jax.random.normal(key_of[2], (SECTIONS, D), jnp.float32), 0.1, 1.9),
        "w_inner": gaussian(key_of[3], (SECTIONS, D, 2 * D), D ** -0.5, 0.1875, ((0, 4),)),
        "w_outer": gaussian(key_of[4], (SECTIONS, D, D), (D // 16) ** -0.5, 0.75, ((0, 4),)),
        "rpe_periods": with_ends(jax.random.randint(key_of[5], (SECTIONS, FREQS), 1, LENGTH // 2), jax.random.fold_in(key_of[5], 1), 1, (LENGTH // 2) - 1).astype(jnp.int32),
        "rpe_in": gaussian(key_of[6], (SECTIONS, 2 * FREQS, RPE), (2 * FREQS) ** -0.5, 0.75, ((0, 4),), jnp.float32),
        "rpe_mid": gaussian(key_of[7], (SECTIONS, RPE, RPE), RPE ** -0.5, 0.75, ((0, 4),), jnp.float32),
        "rpe_out": gaussian(key_of[8], (SECTIONS, RPE, D), (RPE // 16) ** -0.5, 3.0, ((0, 4), (2, 8)), jnp.float32),
        "decay": jnp.clip(jnp.exp(math.log(0.03) - 4.118061 * jax.random.uniform(key_of[9], (SECTIONS, D), jnp.float32) ** steps_of(key_of[9], (SECTIONS, D), ((0, 4), (1, 8)), -0.2, 0.2)), 0.00048828125, 0.03),
    }


EPSILON = 1e-06
PRECISE = lax.Precision.HIGHEST

def kernel_rows(periods, weight_in, weight_mid, weight_out, decay_rate, seq_length):
    positions = jnp.arange(seq_length, dtype=jnp.int32)
    turn_count = periods[:, None] * positions[None, :] % seq_length
    angles = turn_count.astype(jnp.float32) * (2.0 * math.pi / seq_length)
    features = jnp.concatenate([jnp.sin(angles), jnp.cos(angles)], axis=0)
    hidden = jax.nn.relu(jnp.dot(weight_in.T, features, precision=PRECISE))
    hidden = jax.nn.relu(jnp.dot(weight_mid.T, hidden, precision=PRECISE))
    raw_rows = jnp.dot(weight_out.T, hidden, precision=PRECISE)
    place = positions.astype(jnp.float32)
    norm_scale = jnp.sqrt(1.0 - jnp.exp(-2.0 * decay_rate))
    return raw_rows * norm_scale[:, None] * jnp.exp(-decay_rate[:, None] * place[None, :])

def silu_slope(pre_act):
    sigmoid_val = jax.nn.sigmoid(pre_act)
    return sigmoid_val * (1.0 + pre_act * (1.0 - sigmoid_val))

def causal_mix(signal, kernel):
    fft_size = 2 * signal.shape[1]
    product_spec = jnp.fft.rfft(signal, n=fft_size, axis=1) * jnp.fft.rfft(kernel, n=fft_size, axis=1)
    return jnp.fft.irfft(product_spec, n=fft_size, axis=1)[:, :signal.shape[1]]

def reverse_mix(signal, kernel):
    fft_size = 2 * signal.shape[1]
    product_spec = jnp.fft.rfft(signal, n=fft_size, axis=1) * jnp.conj(jnp.fft.rfft(kernel, n=fft_size, axis=1))
    return jnp.fft.irfft(product_spec, n=fft_size, axis=1)[:, :signal.shape[1]]

def forward_values(inputs, gain_row, inner_weight, outer_weight, kernel):
    x_float = inputs.astype(jnp.float32)
    inv_rms = lax.rsqrt(lax.optimization_barrier(jnp.mean(x_float * x_float, axis=1, keepdims=True)) + EPSILON)
    normed = (x_float * inv_rms * gain_row[None, :]).astype(jnp.bfloat16)
    pre_act = jnp.dot(normed, inner_weight, preferred_element_type=jnp.float32)
    gate_act = jax.nn.silu(pre_act[:, :D]).astype(jnp.bfloat16)
    value_act = jax.nn.silu(pre_act[:, D:]).astype(jnp.bfloat16)
    mixed_seq = causal_mix(value_act.T.astype(jnp.float32), kernel).T.astype(jnp.bfloat16)
    gated = (gate_act.astype(jnp.float32) * mixed_seq.astype(jnp.float32)).astype(jnp.bfloat16)
    output = (x_float + jnp.dot(gated, outer_weight, preferred_element_type=jnp.float32)).astype(jnp.bfloat16)
    return (x_float, inv_rms, normed, pre_act, gate_act, mixed_seq, gated, output)

def reference(tokens, cotangent, norm_gain, w_inner, w_outer, rpe_periods, rpe_in, rpe_mid, rpe_out, decay):
    seq_length = tokens.shape[0]
    grad_scale = 1.0 / math.sqrt(seq_length)
    kernels = []
    section_inputs = []
    section_outs = []
    current = tokens
    for section_step in range(SECTIONS):
        kernel = kernel_rows(rpe_periods[section_step], rpe_in[section_step], rpe_mid[section_step], rpe_out[section_step], decay[section_step], seq_length)
        kernels.append(kernel)
        section_inputs.append(current)
        current = forward_values(current, norm_gain[section_step], w_inner[section_step], w_outer[section_step], kernel)[7]
        section_outs.append(current)
    grads_in = [None] * SECTIONS
    inner_grads = [None] * SECTIONS
    outer_grads = [None] * SECTIONS
    grad_now = cotangent
    for section_step in reversed(range(SECTIONS)):
        kernel = kernels[section_step]
        x_float, inv_rms, normed, pre_act, gate_act, mixed_seq, gated, output = forward_values(section_inputs[section_step], norm_gain[section_step], w_inner[section_step], w_outer[section_step], kernel)
        dgated = jnp.dot(grad_now, w_outer[section_step].T, preferred_element_type=jnp.float32)
        dmixed = (dgated * gate_act.astype(jnp.float32)).astype(jnp.bfloat16)
        dgate = dgated * mixed_seq.astype(jnp.float32)
        dvalue = reverse_mix(dmixed.T.astype(jnp.float32), kernel).T.astype(jnp.bfloat16)
        dpre = jnp.concatenate([dgate * silu_slope(pre_act[:, :D]), dvalue.astype(jnp.float32) * silu_slope(pre_act[:, D:])], axis=1).astype(jnp.bfloat16)
        dnormed = jnp.dot(dpre, w_inner[section_step].T, preferred_element_type=jnp.float32)
        dscaled = dnormed * norm_gain[section_step][None, :]
        x_hat = x_float * inv_rms
        shared = lax.optimization_barrier(jnp.mean(dscaled * x_hat, axis=1, keepdims=True))
        grad_in = (grad_now.astype(jnp.float32) + inv_rms * (dscaled - x_hat * shared)).astype(jnp.bfloat16)
        inner_grads[section_step] = jnp.dot(normed.T, dpre, preferred_element_type=jnp.float32) * grad_scale
        outer_grads[section_step] = jnp.dot(gated.T, grad_now, preferred_element_type=jnp.float32) * grad_scale
        grads_in[section_step] = grad_in
        grad_now = grad_in
    return (jnp.stack(section_outs), jnp.stack(grads_in), jnp.stack(inner_grads), jnp.stack(outer_grads))
```

```python
import functools
import math

import jax
import jax.numpy as jnp
import numpy as np
from jax import lax
from jax.experimental import pallas as pl
from jax.experimental.pallas import tpu as pltpu
from jax.sharding import PartitionSpec as P

EPSILON = 1e-06
PRECISE = lax.Precision.HIGHEST


def passed_along(value, axis, steps):
    count = lax.axis_size(axis)
    initial, last = (max(0, -steps), min(count, count - steps))
    return lax.ppermute(value, axis, [(source, source + steps) for source in range(initial, last)])


def kernel_rows(periods, weight_in, weight_mid, weight_out, decay_rate, seq_length):
    positions = jnp.arange(seq_length, dtype=jnp.int32)
    turn_count = periods[:, None] * positions[None, :] % seq_length
    angles = turn_count.astype(jnp.float32) * (2.0 * math.pi / seq_length)
    features = jnp.concatenate([jnp.sin(angles), jnp.cos(angles)], axis=0)
    hidden = jax.nn.relu(jnp.dot(weight_in.T, features, precision=PRECISE))
    hidden = jax.nn.relu(jnp.dot(weight_mid.T, hidden, precision=PRECISE))
    raw_rows = jnp.dot(weight_out.T, hidden, precision=PRECISE)
    place = positions.astype(jnp.float32)
    norm_scale = jnp.sqrt(1.0 - jnp.exp(-2.0 * decay_rate))
    return raw_rows * norm_scale[:, None] * jnp.exp(-decay_rate[:, None] * place[None, :])


def silu_slope(pre_act):
    sigmoid_val = jax.nn.sigmoid(pre_act)
    return sigmoid_val * (1.0 + pre_act * (1.0 - sigmoid_val))


def split_size(fft_size):
    return math.gcd(fft_size, 1 << (fft_size.bit_length() - 1) // 2)


def dft_table(length, sign_value):
    indices = jnp.arange(length, dtype=jnp.int32)
    turn_count = indices[:, None] * indices[None, :] % length
    angles = turn_count.astype(jnp.float32) * (sign_value * 2.0 * math.pi / length)
    return (jnp.cos(angles), jnp.sin(angles))


def twiddle_table(count_rows, count_cols, sign_value):
    fft_size = count_rows * count_cols
    turn_count = (
        jnp.arange(count_rows, dtype=jnp.int32)[:, None]
        * jnp.arange(count_cols, dtype=jnp.int32)[None, :]
    )
    angles = turn_count.astype(jnp.float32) * (sign_value * 2.0 * math.pi / fft_size)
    return (jnp.cos(angles), jnp.sin(angles))


def half_table(size_second):
    half_cols = size_second // 2
    turn_count = (
        jnp.arange(half_cols, dtype=jnp.int32)[:, None]
        * jnp.arange(size_second, dtype=jnp.int32)[None, :]
        % size_second
    )
    angles = turn_count.astype(jnp.float32) * (2.0 * math.pi / size_second)
    return (jnp.cos(angles), jnp.sin(angles))


def parity_signs(size_second):
    return 1.0 - 2.0 * (jnp.arange(size_second, dtype=jnp.int32) % 2).astype(jnp.float32)


def spectrum(signal, size_first):
    own_chans, seq_length = signal.shape
    fft_size = 2 * seq_length
    size_second = fft_size // size_first
    half_rows = size_first // 2
    shaped = signal.reshape(own_chans, half_rows, size_second)
    first_re, first_im = dft_table(size_first, -1.0)
    first_both = jnp.concatenate([first_re[:, :half_rows], first_im[:, :half_rows]], axis=0)
    section = jnp.einsum("kp,cpq->ckq", first_both, shaped, precision=PRECISE)
    section_re = section[:, :size_first]
    section_im = section[:, size_first:]
    twist_re, twist_im = twiddle_table(size_first, size_second, -1.0)
    turned = jnp.concatenate(
        [
            section_re * twist_re - section_im * twist_im,
            section_re * twist_im + section_im * twist_re,
        ],
        axis=2,
    )
    cos_rows, sin_rows = half_table(size_second)
    cos_cols = cos_rows.T
    sin_cols = sin_rows.T
    second_both = jnp.concatenate(
        [
            jnp.concatenate([cos_cols, -sin_cols], axis=1),
            jnp.concatenate([sin_cols, cos_cols], axis=1),
        ],
        axis=0,
    )
    spec = jnp.einsum("ckq,qm->ckm", turned, second_both, precision=PRECISE)
    nyquist = jnp.einsum("cpq,q->c", shaped, parity_signs(size_second), precision=PRECISE)
    return (spec, nyquist[:, None])


def to_signal(spec, nyquist, size_first):
    own_chans, _, size_second = spec.shape
    half_cols = size_second // 2
    half_rows = size_first // 2
    fft_size = size_first * size_second
    row_ids = jnp.arange(size_first, dtype=jnp.int32)[:, None]
    col_ids = jnp.arange(half_cols, dtype=jnp.int32)[None, :]
    weights = jnp.where((row_ids == 0) & (col_ids == 0), 1.0, 2.0).astype(jnp.float32)
    weighted = spec * jnp.concatenate([weights, weights], axis=1)
    cos_rows, sin_rows = half_table(size_second)
    inner_both = jnp.concatenate(
        [
            jnp.concatenate([cos_rows, sin_rows], axis=1),
            jnp.concatenate([-sin_rows, cos_rows], axis=1),
        ],
        axis=0,
    )
    section = jnp.einsum("ckm,mq->ckq", weighted, inner_both, precision=PRECISE)
    section_re = section[:, :, :size_second]
    section_im = section[:, :, size_second:]
    twist_re, twist_im = twiddle_table(size_first, size_second, 1.0)
    turned = jnp.concatenate(
        [
            section_re * twist_re - section_im * twist_im,
            section_re * twist_im + section_im * twist_re,
        ],
        axis=1,
    )
    first_re, first_im = dft_table(size_first, 1.0)
    outer_both = jnp.concatenate([first_re[:half_rows], -first_im[:half_rows]], axis=1)
    signal = jnp.einsum("pk,ckq->cpq", outer_both, turned, precision=PRECISE)
    signal = signal + nyquist[:, :, None] * parity_signs(size_second)[None, None, :]
    return (signal / fft_size).reshape(own_chans, half_rows * size_second)


def on_device_factored(
    tokens, cotangent, norm_gain, w_inner, w_outer, rpe_periods, rpe_in, rpe_mid, rpe_out, decay
):
    tok_rows, model_width = tokens.shape
    seq_parts = lax.axis_size("seq")
    seq_length = tok_rows * seq_parts
    own_chans = model_width // seq_parts
    fft_size = 2 * seq_length
    size_first = split_size(fft_size)
    half_cols = fft_size // size_first // 2
    section_index = lax.axis_index("section")
    section_count = lax.axis_size("section")
    grad_scale = 1.0 / math.sqrt(seq_length)
    gain_row = norm_gain[0]
    inner_weight = w_inner[0]
    outer_weight = w_outer[0]

    def to_channels(block):
        return lax.all_to_all(block, "seq", split_axis=0, concat_axis=1, tiled=True)

    def to_tokens(block):
        return lax.all_to_all(block, "seq", split_axis=1, concat_axis=0, tiled=True)

    def pass_section(block, offset):
        return passed_along(block, "section", offset)

    def token_front(inputs):
        x_float = inputs.astype(jnp.float32)
        inv_rms = lax.rsqrt(jnp.mean(x_float * x_float, axis=1, keepdims=True) + EPSILON)
        normed = (x_float * inv_rms * gain_row[None, :]).astype(jnp.bfloat16)
        pre_act = jnp.einsum("td,de->et", normed, inner_weight, preferred_element_type=jnp.float32)
        value_act = jax.nn.silu(pre_act[model_width:]).astype(jnp.bfloat16)
        return (inv_rms, normed, pre_act, value_act)

    kernel = kernel_rows(rpe_periods[0], rpe_in[0], rpe_mid[0], rpe_out[0], decay[0], seq_length)
    forward_spec, forward_nyq = spectrum(kernel, size_first)

    def channel_forward(value_chan):
        value_spec, value_nyq = spectrum(value_chan.astype(jnp.float32), size_first)
        kernel_re = forward_spec[:, :, :half_cols]
        kernel_im = forward_spec[:, :, half_cols:]
        value_re = value_spec[:, :, :half_cols]
        value_im = value_spec[:, :, half_cols:]
        product = jnp.concatenate(
            [
                value_re * kernel_re - value_im * kernel_im,
                value_re * kernel_im + value_im * kernel_re,
            ],
            axis=2,
        )
        mixed_chan = to_signal(product, value_nyq * forward_nyq, size_first)
        return mixed_chan.astype(jnp.bfloat16)

    def token_back(inputs, pre_act, mixed_tok):
        gate_act = jax.nn.silu(pre_act[:model_width]).astype(jnp.bfloat16)
        gated = (gate_act.astype(jnp.float32) * mixed_tok.astype(jnp.float32)).astype(jnp.bfloat16)
        update = jnp.einsum("et,ef->tf", gated, outer_weight, preferred_element_type=jnp.float32)
        return (gated, (inputs.astype(jnp.float32) + update).astype(jnp.bfloat16))

    zero_tok = jnp.zeros((tok_rows, model_width), jnp.bfloat16)
    zero_cols = jnp.zeros((model_width, tok_rows), jnp.bfloat16)
    zero_chan = jnp.zeros((own_chans, seq_length), jnp.bfloat16)
    current = tokens
    kept_input = zero_tok
    kept_front = (
        jnp.zeros((tok_rows, 1), jnp.float32),
        zero_tok,
        jnp.zeros((2 * model_width, tok_rows), jnp.float32),
        zero_cols,
    )
    kept_mixed = zero_cols
    kept_gated = zero_cols
    produced = zero_tok
    for section_step in range(section_count):
        active = section_index == section_step
        source = current
        kept_input = jnp.where(active, source, kept_input)
        kept_front = lax.cond(
            active, lambda: token_front(source), lambda previous=kept_front: previous
        )
        value_chan = to_channels(kept_front[3])
        mixed_chan = lax.cond(active, lambda: channel_forward(value_chan), lambda: zero_chan)
        mixed_tok = to_tokens(mixed_chan)
        kept_mixed = jnp.where(active, mixed_tok, kept_mixed)
        front_now = kept_front
        kept_gated, produced = lax.cond(
            active,
            lambda: token_back(source, front_now[2], mixed_tok),
            lambda previous=(kept_gated, produced): previous,
        )
        if section_step + 1 < section_count:
            current = pass_section(produced, 1)
    inv_rms, normed, pre_act, value_act = kept_front
    backward_spec, backward_nyq = (forward_spec, forward_nyq)

    def grad_front(grad_out):
        dgated = jnp.einsum("tf,ef->et", grad_out, outer_weight, preferred_element_type=jnp.float32)
        gate_act = jax.nn.silu(pre_act[:model_width]).astype(jnp.bfloat16)
        dmixed = (dgated * gate_act.astype(jnp.float32)).astype(jnp.bfloat16)
        return (dmixed, dgated * kept_mixed.astype(jnp.float32))

    def channel_backward(dmixed_chan):
        kernel_re = backward_spec[:, :, :half_cols]
        kernel_im = backward_spec[:, :, half_cols:]
        grad_spec, grad_nyq = spectrum(dmixed_chan.astype(jnp.float32), size_first)
        grad_re = grad_spec[:, :, :half_cols]
        grad_im = grad_spec[:, :, half_cols:]
        product = jnp.concatenate(
            [grad_re * kernel_re + grad_im * kernel_im, grad_im * kernel_re - grad_re * kernel_im],
            axis=2,
        )
        dvalue_chan = to_signal(product, grad_nyq * backward_nyq, size_first)
        return dvalue_chan.astype(jnp.bfloat16)

    def grad_back(dvalue_tok, dgate, grad_out):
        dpre = jnp.concatenate(
            [
                dgate * silu_slope(pre_act[:model_width]),
                dvalue_tok.astype(jnp.float32) * silu_slope(pre_act[model_width:]),
            ],
            axis=0,
        ).astype(jnp.bfloat16)
        dnormed = jnp.einsum("et,de->td", dpre, inner_weight, preferred_element_type=jnp.float32)
        x_float = kept_input.astype(jnp.float32)
        dscaled = dnormed * gain_row[None, :]
        x_hat = x_float * inv_rms
        shared = jnp.mean(dscaled * x_hat, axis=1, keepdims=True)
        grad_in = (grad_out.astype(jnp.float32) + inv_rms * (dscaled - x_hat * shared)).astype(
            jnp.bfloat16
        )
        return (dpre, grad_in)

    grad_now = cotangent
    grad_input = zero_tok
    kept_grad = zero_tok
    kept_dgate = jnp.zeros((model_width, tok_rows), jnp.float32)
    kept_dpre = jnp.zeros((2 * model_width, tok_rows), jnp.bfloat16)
    for section_step in reversed(range(section_count)):
        active = section_index == section_step
        arriving = grad_now
        kept_grad = jnp.where(active, arriving, kept_grad)
        dmixed_tok, kept_dgate = lax.cond(
            active, lambda: grad_front(arriving), lambda previous=kept_dgate: (zero_cols, previous)
        )
        dmixed_chan = to_channels(dmixed_tok)
        dvalue_chan = lax.cond(active, lambda: channel_backward(dmixed_chan), lambda: zero_chan)
        dvalue_tok = to_tokens(dvalue_chan)
        dgate_now = kept_dgate
        kept_dpre, grad_input = lax.cond(
            active,
            lambda: grad_back(dvalue_tok, dgate_now, arriving),
            lambda previous=(kept_dpre, grad_input): previous,
        )
        if section_step > 0:
            grad_now = pass_section(grad_input, -1)
    inner_term = jnp.einsum("tr,et->re", normed, kept_dpre, preferred_element_type=jnp.float32)
    outer_term = jnp.einsum("et,tf->ef", kept_gated, kept_grad, preferred_element_type=jnp.float32)
    inner_sum, outer_sum = (
        lax.psum_scatter(inner_term, "seq", scatter_dimension=0, tiled=True),
        lax.psum_scatter(outer_term, "seq", scatter_dimension=0, tiled=True),
    )
    return (
        produced[None],
        grad_input[None],
        (inner_sum * grad_scale)[None],
        (outer_sum * grad_scale)[None],
    )


def dense_tables(seq_length):
    fft_size = 2 * seq_length
    coarse = math.gcd(seq_length, 32)
    fine = seq_length // coarse
    place = np.arange(seq_length, dtype=np.int64)

    def pair(freqs):
        angles = 2.0 * np.pi / fft_size * (freqs[:, None] * place[None, :] % fft_size)
        return (np.cos(angles).astype(np.float32), np.sin(angles).astype(np.float32))

    high_cos, high_sin = pair(np.arange(coarse, dtype=np.int64) * fine)
    low_cos, low_sin = pair(np.arange(fine, dtype=np.int64))
    parity = (1.0 - 2.0 * (place % 2)).astype(np.float32)

    def build(high, low, shape, freq_axis):
        hc, hs = high
        lc, ls = low
        cos = (hc * lc - hs * ls).reshape(shape)
        sin = -(hs * lc + hc * ls).reshape(shape)
        freq = lax.broadcasted_iota(jnp.int32, shape, freq_axis)
        signs = parity[None, :] if freq_axis == 0 else parity[:, None]
        sin = jnp.where(freq == 0, signs, sin)
        return jnp.concatenate([cos, sin], axis=freq_axis).astype(jnp.bfloat16)

    analysis = build(
        (jnp.asarray(high_cos)[:, None, :], jnp.asarray(high_sin)[:, None, :]),
        (jnp.asarray(low_cos)[None], jnp.asarray(low_sin)[None]),
        (seq_length, seq_length),
        0,
    )
    return analysis


def silu_pair(pre_act):
    sigmoid_val = 1.0 / (1.0 + jnp.exp(-pre_act))
    return pre_act * sigmoid_val, sigmoid_val * (1.0 + pre_act * (1.0 - sigmoid_val))


def relay_kernel(
    parts,
    sections,
    tok_ref,
    cot_ref,
    gain_ref,
    wi_ref,
    wo_ref,
    ana_ref,
    syn_ref,
    spec_ref,
    out_ref,
    gin_ref,
    res_ref,
    xbuf,
    gbuf,
    gate_act,
    gate_slope,
    val_slope,
    send_a,
    chan_a,
    zbuf,
    mix_chan,
    mix_tok,
    send_b,
    chan_b,
    dval_chan,
    dval_tok,
    dgate_send,
    dgate_chan,
    arr_chan,
    slope_chan,
    normed_all,
    gated_all,
    res_send,
    a2a_send,
    a2a_recv,
    own_sem,
    gat_send,
    gat_recv,
    fwd_send,
    fwd_recv,
    hop_send,
    hop_recv,
):
    f32, bf16 = jnp.float32, jnp.bfloat16
    sec = lax.axis_index("section")
    me = lax.axis_index("seq")
    rows, width = tok_ref.shape
    length = rows * parts
    cols = width // parts

    def ds(index, size):
        return pl.ds(pl.multiple_of(index * size, size), size)

    def peer(step):
        return lax.rem(me + step, parts)

    barrier = pltpu.get_barrier_semaphore()
    for step in range(1, parts):
        pl.semaphore_signal(barrier, inc=1, device_id={"seq": peer(step)})

    for step in (1, sections - 1):
        pl.semaphore_signal(
            barrier, inc=1, device_id={"section": lax.rem(sec + step, sections)}
        )
    pl.semaphore_wait(barrier, parts + 1)

    def exchange(slot, source, target):
        copies = []
        for step in range(1, parts):
            copies.append(
                pltpu.make_async_remote_copy(
                    src_ref=source(peer(step)),
                    dst_ref=target(me),
                    send_sem=a2a_send.at[slot, step],
                    recv_sem=a2a_recv.at[slot, step],
                    device_id={"seq": peer(step)},
                )
            )
        copies.append(pltpu.make_async_copy(source(me), target(me), own_sem.at[slot]))
        return copies

    def start(copies):
        for copy in copies:
            copy.start()

    def arrive(copies):
        for copy in copies[:-1]:
            copy.wait_recv()
        copies[-1].wait()

    def left(copies):
        for copy in copies[:-1]:
            copy.wait_send()

    def col_block(ref):
        return lambda device: ref.at[:, ds(device, cols)]

    def row_block(ref, size):
        return lambda device: ref.at[ds(device, size), :]

    def mix(source, target, sign):
        half = spec_ref.shape[1]
        chunk = min(half, 256)
        signal = source[...]
        for first in range(0, half, chunk):
            band = slice(first, first + chunk)
            real = jnp.dot(ana_ref[band, :], signal, preferred_element_type=f32)
            imag = jnp.dot(
                ana_ref[half + first : half + first + chunk, :], signal, preferred_element_type=f32
            )
            k_re, k_im, k_ny = spec_ref[0, band, :], spec_ref[1, band, :], spec_ref[2, band, :]
            zbuf[band, :] = (real * k_re - sign * (imag * k_im)).astype(bf16)
            zbuf[half + first : half + first + chunk, :] = (
                sign * (real * k_im) + imag * k_ny
            ).astype(bf16)
        shaped = zbuf[...]
        for first in range(0, length, chunk):
            target[first : first + chunk, :] = jnp.dot(
                syn_ref[first : first + chunk, :], shaped, preferred_element_type=f32
            ).astype(bf16)

    hop_fwd = pltpu.make_async_remote_copy(
        src_ref=out_ref,
        dst_ref=xbuf,
        send_sem=hop_send.at[0],
        recv_sem=hop_recv.at[0],
        device_id={"section": jnp.minimum(sec + 1, sections - 1)},
    )
    hop_bwd = pltpu.make_async_remote_copy(
        src_ref=gin_ref,
        dst_ref=gbuf,
        send_sem=hop_send.at[1],
        recv_sem=hop_recv.at[1],
        device_id={"section": jnp.maximum(sec - 1, 0)},
    )

    @pl.when(sec == 0)
    def _():
        xbuf[...] = tok_ref[...]

    @pl.when(sec > 0)
    def _():
        hop_fwd.wait_recv()

    gain = gain_ref[...]
    own_rows = ds(me, rows)

    x_float = xbuf[...].astype(f32)
    inv_rms = lax.rsqrt(jnp.mean(x_float * x_float, axis=1, keepdims=True) + EPSILON)
    normed = (x_float * inv_rms * gain).astype(bf16)
    normed_all[own_rows, :] = normed
    pre_val = jnp.dot(normed, wi_ref[:, width:], preferred_element_type=f32)
    act, slope = silu_pair(pre_val)
    send_a[...] = act.astype(bf16)
    to_chan = exchange(0, col_block(send_a), row_block(chan_a, rows))
    start(to_chan)
    val_slope[...] = slope.astype(bf16)
    pre_gate = jnp.dot(normed, wi_ref[:, :width], preferred_element_type=f32)
    act, slope = silu_pair(pre_gate)
    gate_act[...] = act.astype(bf16)
    gate_slope[...] = slope
    arrive(to_chan)
    mix(chan_a, mix_chan, 1.0)
    to_tok = exchange(1, row_block(mix_chan, rows), col_block(mix_tok))
    start(to_tok)
    arrive(to_tok)
    gated = (gate_act[...].astype(f32) * mix_tok[...].astype(f32)).astype(bf16)
    gated_all[own_rows, :] = gated
    update = jnp.dot(gated, wo_ref[...], preferred_element_type=f32)
    out_ref[...] = (xbuf[...].astype(f32) + update).astype(bf16)

    @pl.when(sec < sections - 1)
    def _():
        hop_fwd.start()

    left(to_chan)
    left(to_tok)

    slope_move = exchange(2, col_block(val_slope), row_block(slope_chan, rows))
    partner = me + 1 - 2 * lax.rem(me, 2)
    chips = parts // 2
    far, near = [], []
    for index, ref in enumerate((normed_all, gated_all)):
        for step in range(chips):
            owner = lax.rem(me + parts - 2 * step, parts)
            if step > 0:
                far.append(
                    pltpu.make_async_remote_copy(
                        src_ref=ref.at[own_rows, :],
                        dst_ref=ref.at[own_rows, :],
                        send_sem=gat_send.at[index, step],
                        recv_sem=gat_recv.at[index, step],
                        device_id={"seq": peer(2 * step)},
                    )
                )
            near.append(
                pltpu.make_async_remote_copy(
                    src_ref=ref.at[ds(owner, rows), :],
                    dst_ref=ref.at[ds(owner, rows), :],
                    send_sem=fwd_send.at[index, step],
                    recv_sem=fwd_recv.at[index, step],
                    device_id={"seq": partner},
                )
            )

    def gather():
        start(slope_move)
        start(far)
        for index in range(2):
            near[index * chips].start()
            for step in range(1, chips):
                far[index * (chips - 1) + step - 1].wait_recv()
                near[index * chips + step].start()
        for copy in near:
            copy.wait()
        for copy in far:
            copy.wait_send()
        arrive(slope_move)
        left(slope_move)

    early = sections // 2

    @pl.when(sec < early)
    def _():
        gather()

    @pl.when(sec == sections - 1)
    def _():
        gbuf[...] = cot_ref[...]

    @pl.when(sec < sections - 1)
    def _():
        hop_bwd.wait_recv()

    contract_last = (((1,), (1,)), ((), ()))
    contract_first = (((0,), (0,)), ((), ()))
    dgated = lax.dot_general(gbuf[...], wo_ref[...], contract_last, preferred_element_type=f32)
    send_b[...] = (dgated * gate_act[...].astype(f32)).astype(bf16)
    grad_chan = exchange(3, col_block(send_b), row_block(chan_b, rows))
    start(grad_chan)
    dpre_gate = (dgated * mix_tok[...].astype(f32) * gate_slope[...]).astype(bf16)
    dgate_send[...] = dpre_gate
    dnormed_gate = lax.dot_general(
        dpre_gate, wi_ref[:, :width], contract_last, preferred_element_type=f32
    )
    arrive(grad_chan)
    arr_move = exchange(4, col_block(gbuf), row_block(arr_chan, rows))
    dgate_move = exchange(5, col_block(dgate_send), row_block(dgate_chan, rows))
    mix(chan_b, dval_chan, -1.0)
    grad_tok = exchange(6, row_block(dval_chan, rows), col_block(dval_tok))
    start(grad_tok)
    start(arr_move)
    start(dgate_move)

    def result(part, lhs, rhs):
        piece = lax.dot_general(lhs, rhs[...], contract_first, preferred_element_type=f32)
        res_send[part] = piece.astype(bf16)

    arrive(grad_tok)
    dpre_val = (dval_tok[...].astype(f32) * val_slope[...].astype(f32)).astype(bf16)
    dnormed = dnormed_gate + lax.dot_general(
        dpre_val, wi_ref[:, width:], contract_last, preferred_element_type=f32
    )
    x_float = xbuf[...].astype(f32)
    inv_rms = lax.rsqrt(jnp.mean(x_float * x_float, axis=1, keepdims=True) + EPSILON)
    dscaled = dnormed * gain
    x_hat = x_float * inv_rms
    shared = jnp.mean(dscaled * x_hat, axis=1, keepdims=True)
    gin_ref[...] = (gbuf[...].astype(f32) + inv_rms * (dscaled - x_hat * shared)).astype(bf16)

    @pl.when(sec > 0)
    def _():
        hop_bwd.start()

    @pl.when(sec >= early)
    def _():
        gather()

    moves = []
    for part in range(3):
        if part == 0:
            dval = (dval_chan[...].astype(f32) * slope_chan[...].astype(f32)).astype(bf16)
            result(0, dval, normed_all)
        elif part == 1:
            arrive(arr_move)
            result(1, arr_chan[...], gated_all)
        else:
            arrive(dgate_move)
            result(2, dgate_chan[...], normed_all)
        move = exchange(
            7 + part,
            lambda device, part=part: res_send.at[part, :, ds(device, cols)],
            lambda device, part=part: res_ref.at[part, ds(device, cols), :],
        )
        start(move)
        moves.append(move)
    for move in moves:
        arrive(move)
        left(move)
    for move in (grad_chan, grad_tok, arr_move, dgate_move):
        left(move)

    @pl.when(sec < sections - 1)
    def _():
        hop_fwd.wait_send()

    @pl.when(sec > 0)
    def _():
        hop_bwd.wait_send()


def on_device(
    tokens, cotangent, norm_gain, w_inner, w_outer, rpe_periods, rpe_in, rpe_mid, rpe_out, decay
):
    rows, width = tokens.shape
    parts = lax.axis_size("seq")
    sections = lax.axis_size("section")
    cols = width // parts
    length = rows * parts
    if cols % 128 or rows % 128 or length > 1024 or parts % 2 or sections < 2:
        return on_device_factored(
            tokens, cotangent, norm_gain, w_inner, w_outer, rpe_periods, rpe_in, rpe_mid, rpe_out, decay
        )
    bf16, f32 = jnp.bfloat16, jnp.float32
    analysis = lax.optimization_barrier(dense_tables(length))
    synthesis = analysis.T
    kernel = kernel_rows(rpe_periods[0], rpe_in[0], rpe_mid[0], rpe_out[0], decay[0], length)
    spec = lax.dot_general(
        analysis, kernel.astype(bf16), (((1,), (1,)), ((), ())), preferred_element_type=f32
    )
    first = lax.broadcasted_iota(jnp.int32, (length, 1), 0) == 0
    scale = jnp.where(first, 0.5, 1.0) / length
    real, imag = spec[:length] * scale, spec[length:] * scale
    spec = jnp.stack([real, jnp.where(first, 0.0, imag), jnp.where(first, imag, real)])
    tok_block = lambda kind: pltpu.VMEM((rows, width), kind)
    chan_block = lambda kind: pltpu.VMEM((length, cols), kind)
    vmem = pl.BlockSpec(memory_space=pltpu.VMEM)
    dma = pltpu.SemaphoreType.DMA
    out, grad_in, res = pl.pallas_call(
        functools.partial(relay_kernel, parts, sections),
        out_shape=(
            jax.ShapeDtypeStruct((rows, width), bf16),
            jax.ShapeDtypeStruct((rows, width), bf16),
            jax.ShapeDtypeStruct((3, width, cols), bf16),
        ),
        in_specs=[vmem] * 8,
        out_specs=(vmem,) * 3,
        scratch_shapes=[
            tok_block(bf16),
            tok_block(bf16),
            tok_block(bf16),
            tok_block(f32),
            tok_block(bf16),
            tok_block(bf16),
            chan_block(bf16),
            pltpu.VMEM((2 * length, cols), bf16),
            chan_block(bf16),
            tok_block(bf16),
            tok_block(bf16),
            chan_block(bf16),
            chan_block(bf16),
            tok_block(bf16),
            tok_block(bf16),
            chan_block(bf16),
            chan_block(bf16),
            chan_block(bf16),
            pltpu.VMEM((length, width), bf16),
            pltpu.VMEM((length, width), bf16),
            pltpu.VMEM((3, cols, width), bf16),
            dma((10, parts)),
            dma((10, parts)),
            dma((10,)),
            dma((2, parts // 2)),
            dma((2, parts // 2)),
            dma((2, parts // 2)),
            dma((2, parts // 2)),
            dma((2,)),
            dma((2,)),
        ],
        compiler_params=pltpu.CompilerParams(
            collective_id=0, has_side_effects=True, vmem_limit_bytes=60 * 1024 * 1024
        ),
    )(
        tokens,
        cotangent,
        norm_gain,
        w_inner[0],
        w_outer[0],
        analysis,
        synthesis,
        spec,
    )
    grad_scale = 1.0 / math.sqrt(length)
    inner = jnp.concatenate([res[2], res[0]], axis=0).T.astype(f32) * grad_scale
    outer = res[1].T.astype(f32) * grad_scale
    return (out[None], grad_in[None], inner[None], outer[None])


def solution(mesh):
    return jax.shard_map(
        on_device,
        mesh=mesh,
        in_specs=(
            P("seq", None),
            P("seq", None),
            P("section", None),
            P("section", None, None),
            P("section", None, None),
            P("section", None),
            P("section", None, None),
            P("section", None, None),
            P("section", None, "seq"),
            P("section", "seq"),
        ),
        out_specs=(
            P("section", "seq", None),
            P("section", "seq", None),
            P("section", "seq", None),
            P("section", "seq", None),
        ),
        check_vma=False,
    )
```

```python
import functools
import math

import jax
import jax.numpy as jnp
import numpy as np
from jax import lax
from jax.experimental import pallas as pl
from jax.experimental.pallas import tpu as pltpu
from jax.sharding import PartitionSpec as P

EPSILON = 1e-06
PRECISE = lax.Precision.HIGHEST


def passed_along(value, axis, steps):
    count = lax.axis_size(axis)
    initial, last = (max(0, -steps), min(count, count - steps))
    return lax.ppermute(value, axis, [(source, source + steps) for source in range(initial, last)])


def kernel_rows(periods, weight_in, weight_mid, weight_out, decay_rate, seq_length):
    positions = jnp.arange(seq_length, dtype=jnp.int32)
    turn_count = periods[:, None] * positions[None, :] % seq_length
    angles = turn_count.astype(jnp.float32) * (2.0 * math.pi / seq_length)
    features = jnp.concatenate([jnp.sin(angles), jnp.cos(angles)], axis=0)
    hidden = jax.nn.relu(jnp.dot(weight_in.T, features, precision=PRECISE))
    hidden = jax.nn.relu(jnp.dot(weight_mid.T, hidden, precision=PRECISE))
    raw_rows = jnp.dot(weight_out.T, hidden, precision=PRECISE)
    place = positions.astype(jnp.float32)
    norm_scale = jnp.sqrt(1.0 - jnp.exp(-2.0 * decay_rate))
    return raw_rows * norm_scale[:, None] * jnp.exp(-decay_rate[:, None] * place[None, :])


def silu_slope(pre_act):
    sigmoid_val = jax.nn.sigmoid(pre_act)
    return sigmoid_val * (1.0 + pre_act * (1.0 - sigmoid_val))


def split_size(fft_size):
    return math.gcd(fft_size, 1 << (fft_size.bit_length() - 1) // 2)


def dft_table(length, sign_value):
    indices = jnp.arange(length, dtype=jnp.int32)
    turn_count = indices[:, None] * indices[None, :] % length
    angles = turn_count.astype(jnp.float32) * (sign_value * 2.0 * math.pi / length)
    return (jnp.cos(angles), jnp.sin(angles))


def twiddle_table(count_rows, count_cols, sign_value):
    fft_size = count_rows * count_cols
    turn_count = (
        jnp.arange(count_rows, dtype=jnp.int32)[:, None]
        * jnp.arange(count_cols, dtype=jnp.int32)[None, :]
    )
    angles = turn_count.astype(jnp.float32) * (sign_value * 2.0 * math.pi / fft_size)
    return (jnp.cos(angles), jnp.sin(angles))


def half_table(size_second):
    half_cols = size_second // 2
    turn_count = (
        jnp.arange(half_cols, dtype=jnp.int32)[:, None]
        * jnp.arange(size_second, dtype=jnp.int32)[None, :]
        % size_second
    )
    angles = turn_count.astype(jnp.float32) * (2.0 * math.pi / size_second)
    return (jnp.cos(angles), jnp.sin(angles))


def parity_signs(size_second):
    return 1.0 - 2.0 * (jnp.arange(size_second, dtype=jnp.int32) % 2).astype(jnp.float32)


def spectrum(signal, size_first):
    own_chans, seq_length = signal.shape
    fft_size = 2 * seq_length
    size_second = fft_size // size_first
    half_rows = size_first // 2
    shaped = signal.reshape(own_chans, half_rows, size_second)
    first_re, first_im = dft_table(size_first, -1.0)
    first_both = jnp.concatenate([first_re[:, :half_rows], first_im[:, :half_rows]], axis=0)
    section = jnp.einsum("kp,cpq->ckq", first_both, shaped, precision=PRECISE)
    section_re = section[:, :size_first]
    section_im = section[:, size_first:]
    twist_re, twist_im = twiddle_table(size_first, size_second, -1.0)
    turned = jnp.concatenate(
        [
            section_re * twist_re - section_im * twist_im,
            section_re * twist_im + section_im * twist_re,
        ],
        axis=2,
    )
    cos_rows, sin_rows = half_table(size_second)
    cos_cols = cos_rows.T
    sin_cols = sin_rows.T
    second_both = jnp.concatenate(
        [
            jnp.concatenate([cos_cols, -sin_cols], axis=1),
            jnp.concatenate([sin_cols, cos_cols], axis=1),
        ],
        axis=0,
    )
    spec = jnp.einsum("ckq,qm->ckm", turned, second_both, precision=PRECISE)
    nyquist = jnp.einsum("cpq,q->c", shaped, parity_signs(size_second), precision=PRECISE)
    return (spec, nyquist[:, None])


def to_signal(spec, nyquist, size_first):
    own_chans, _, size_second = spec.shape
    half_cols = size_second // 2
    half_rows = size_first // 2
    fft_size = size_first * size_second
    row_ids = jnp.arange(size_first, dtype=jnp.int32)[:, None]
    col_ids = jnp.arange(half_cols, dtype=jnp.int32)[None, :]
    weights = jnp.where((row_ids == 0) & (col_ids == 0), 1.0, 2.0).astype(jnp.float32)
    weighted = spec * jnp.concatenate([weights, weights], axis=1)
    cos_rows, sin_rows = half_table(size_second)
    inner_both = jnp.concatenate(
        [
            jnp.concatenate([cos_rows, sin_rows], axis=1),
            jnp.concatenate([-sin_rows, cos_rows], axis=1),
        ],
        axis=0,
    )
    section = jnp.einsum("ckm,mq->ckq", weighted, inner_both, precision=PRECISE)
    section_re = section[:, :, :size_second]
    section_im = section[:, :, size_second:]
    twist_re, twist_im = twiddle_table(size_first, size_second, 1.0)
    turned = jnp.concatenate(
        [
            section_re * twist_re - section_im * twist_im,
            section_re * twist_im + section_im * twist_re,
        ],
        axis=1,
    )
    first_re, first_im = dft_table(size_first, 1.0)
    outer_both = jnp.concatenate([first_re[:half_rows], -first_im[:half_rows]], axis=1)
    signal = jnp.einsum("pk,ckq->cpq", outer_both, turned, precision=PRECISE)
    signal = signal + nyquist[:, :, None] * parity_signs(size_second)[None, None, :]
    return (signal / fft_size).reshape(own_chans, half_rows * size_second)


def on_device_factored(
    tokens, cotangent, norm_gain, w_inner, w_outer, rpe_periods, rpe_in, rpe_mid, rpe_out, decay
):
    tok_rows, model_width = tokens.shape
    seq_parts = lax.axis_size("seq")
    seq_length = tok_rows * seq_parts
    own_chans = model_width // seq_parts
    fft_size = 2 * seq_length
    size_first = split_size(fft_size)
    half_cols = fft_size // size_first // 2
    section_index = lax.axis_index("section")
    section_count = lax.axis_size("section")
    grad_scale = 1.0 / math.sqrt(seq_length)
    gain_row = norm_gain[0]
    inner_weight = w_inner[0]
    outer_weight = w_outer[0]

    def to_channels(block):
        return lax.all_to_all(block, "seq", split_axis=0, concat_axis=1, tiled=True)

    def to_tokens(block):
        return lax.all_to_all(block, "seq", split_axis=1, concat_axis=0, tiled=True)

    def pass_section(block, offset):
        return passed_along(block, "section", offset)

    def token_front(inputs):
        x_float = inputs.astype(jnp.float32)
        inv_rms = lax.rsqrt(jnp.mean(x_float * x_float, axis=1, keepdims=True) + EPSILON)
        normed = (x_float * inv_rms * gain_row[None, :]).astype(jnp.bfloat16)
        pre_act = jnp.einsum("td,de->et", normed, inner_weight, preferred_element_type=jnp.float32)
        value_act = jax.nn.silu(pre_act[model_width:]).astype(jnp.bfloat16)
        return (inv_rms, normed, pre_act, value_act)

    kernel = kernel_rows(rpe_periods[0], rpe_in[0], rpe_mid[0], rpe_out[0], decay[0], seq_length)
    forward_spec, forward_nyq = spectrum(kernel, size_first)

    def channel_forward(value_chan):
        value_spec, value_nyq = spectrum(value_chan.astype(jnp.float32), size_first)
        kernel_re = forward_spec[:, :, :half_cols]
        kernel_im = forward_spec[:, :, half_cols:]
        value_re = value_spec[:, :, :half_cols]
        value_im = value_spec[:, :, half_cols:]
        product = jnp.concatenate(
            [
                value_re * kernel_re - value_im * kernel_im,
                value_re * kernel_im + value_im * kernel_re,
            ],
            axis=2,
        )
        mixed_chan = to_signal(product, value_nyq * forward_nyq, size_first)
        return mixed_chan.astype(jnp.bfloat16)

    def token_back(inputs, pre_act, mixed_tok):
        gate_act = jax.nn.silu(pre_act[:model_width]).astype(jnp.bfloat16)
        gated = (gate_act.astype(jnp.float32) * mixed_tok.astype(jnp.float32)).astype(jnp.bfloat16)
        update = jnp.einsum("et,ef->tf", gated, outer_weight, preferred_element_type=jnp.float32)
        return (gated, (inputs.astype(jnp.float32) + update).astype(jnp.bfloat16))

    zero_tok = jnp.zeros((tok_rows, model_width), jnp.bfloat16)
    zero_cols = jnp.zeros((model_width, tok_rows), jnp.bfloat16)
    zero_chan = jnp.zeros((own_chans, seq_length), jnp.bfloat16)
    current = tokens
    kept_input = zero_tok
    kept_front = (
        jnp.zeros((tok_rows, 1), jnp.float32),
        zero_tok,
        jnp.zeros((2 * model_width, tok_rows), jnp.float32),
        zero_cols,
    )
    kept_mixed = zero_cols
    kept_gated = zero_cols
    produced = zero_tok
    for section_step in range(section_count):
        active = section_index == section_step
        source = current
        kept_input = jnp.where(active, source, kept_input)
        kept_front = lax.cond(
            active, lambda: token_front(source), lambda previous=kept_front: previous
        )
        value_chan = to_channels(kept_front[3])
        mixed_chan = lax.cond(active, lambda: channel_forward(value_chan), lambda: zero_chan)
        mixed_tok = to_tokens(mixed_chan)
        kept_mixed = jnp.where(active, mixed_tok, kept_mixed)
        front_now = kept_front
        kept_gated, produced = lax.cond(
            active,
            lambda: token_back(source, front_now[2], mixed_tok),
            lambda previous=(kept_gated, produced): previous,
        )
        if section_step + 1 < section_count:
            current = pass_section(produced, 1)
    inv_rms, normed, pre_act, value_act = kept_front
    backward_spec, backward_nyq = (forward_spec, forward_nyq)

    def grad_front(grad_out):
        dgated = jnp.einsum("tf,ef->et", grad_out, outer_weight, preferred_element_type=jnp.float32)
        gate_act = jax.nn.silu(pre_act[:model_width]).astype(jnp.bfloat16)
        dmixed = (dgated * gate_act.astype(jnp.float32)).astype(jnp.bfloat16)
        return (dmixed, dgated * kept_mixed.astype(jnp.float32))

    def channel_backward(dmixed_chan):
        kernel_re = backward_spec[:, :, :half_cols]
        kernel_im = backward_spec[:, :, half_cols:]
        grad_spec, grad_nyq = spectrum(dmixed_chan.astype(jnp.float32), size_first)
        grad_re = grad_spec[:, :, :half_cols]
        grad_im = grad_spec[:, :, half_cols:]
        product = jnp.concatenate(
            [grad_re * kernel_re + grad_im * kernel_im, grad_im * kernel_re - grad_re * kernel_im],
            axis=2,
        )
        dvalue_chan = to_signal(product, grad_nyq * backward_nyq, size_first)
        return dvalue_chan.astype(jnp.bfloat16)

    def grad_back(dvalue_tok, dgate, grad_out):
        dpre = jnp.concatenate(
            [
                dgate * silu_slope(pre_act[:model_width]),
                dvalue_tok.astype(jnp.float32) * silu_slope(pre_act[model_width:]),
            ],
            axis=0,
        ).astype(jnp.bfloat16)
        dnormed = jnp.einsum("et,de->td", dpre, inner_weight, preferred_element_type=jnp.float32)
        x_float = kept_input.astype(jnp.float32)
        dscaled = dnormed * gain_row[None, :]
        x_hat = x_float * inv_rms
        shared = jnp.mean(dscaled * x_hat, axis=1, keepdims=True)
        grad_in = (grad_out.astype(jnp.float32) + inv_rms * (dscaled - x_hat * shared)).astype(
            jnp.bfloat16
        )
        return (dpre, grad_in)

    grad_now = cotangent
    grad_input = zero_tok
    kept_grad = zero_tok
    kept_dgate = jnp.zeros((model_width, tok_rows), jnp.float32)
    kept_dpre = jnp.zeros((2 * model_width, tok_rows), jnp.bfloat16)
    for section_step in reversed(range(section_count)):
        active = section_index == section_step
        arriving = grad_now
        kept_grad = jnp.where(active, arriving, kept_grad)
        dmixed_tok, kept_dgate = lax.cond(
            active, lambda: grad_front(arriving), lambda previous=kept_dgate: (zero_cols, previous)
        )
        dmixed_chan = to_channels(dmixed_tok)
        dvalue_chan = lax.cond(active, lambda: channel_backward(dmixed_chan), lambda: zero_chan)
        dvalue_tok = to_tokens(dvalue_chan)
        dgate_now = kept_dgate
        kept_dpre, grad_input = lax.cond(
            active,
            lambda: grad_back(dvalue_tok, dgate_now, arriving),
            lambda previous=(kept_dpre, grad_input): previous,
        )
        if section_step > 0:
            grad_now = pass_section(grad_input, -1)
    inner_term = jnp.einsum("tr,et->re", normed, kept_dpre, preferred_element_type=jnp.float32)
    outer_term = jnp.einsum("et,tf->ef", kept_gated, kept_grad, preferred_element_type=jnp.float32)
    inner_sum, outer_sum = (
        lax.psum_scatter(inner_term, "seq", scatter_dimension=0, tiled=True),
        lax.psum_scatter(outer_term, "seq", scatter_dimension=0, tiled=True),
    )
    return (
        produced[None],
        grad_input[None],
        (inner_sum * grad_scale)[None],
        (outer_sum * grad_scale)[None],
    )


SPLITS = 2


def dense_tables(seq_length):
    fft_size = 2 * seq_length
    coarse = math.gcd(seq_length, 32)
    fine = seq_length // coarse
    place = np.arange(seq_length, dtype=np.int64)

    def pair(freqs):
        angles = 2.0 * np.pi / fft_size * (freqs[:, None] * place[None, :] % fft_size)
        return (np.cos(angles).astype(np.float32), np.sin(angles).astype(np.float32))

    high_cos, high_sin = pair(np.arange(coarse, dtype=np.int64) * fine)
    low_cos, low_sin = pair(np.arange(fine, dtype=np.int64))
    parity = np.broadcast_to((1.0 - 2.0 * (place % 2)).astype(np.float32), (16, seq_length))
    shape = (seq_length, seq_length)
    hc, hs = jnp.asarray(high_cos)[:, None, :], jnp.asarray(high_sin)[:, None, :]
    lc, ls = jnp.asarray(low_cos)[None], jnp.asarray(low_sin)[None]
    cos = (hc * lc - hs * ls).reshape(shape).astype(jnp.bfloat16)
    sin = (-(hs * lc + hc * ls)).reshape(shape).astype(jnp.bfloat16)
    return cos, sin, jnp.asarray(parity).astype(jnp.bfloat16)


def silu_pair(pre_act):
    sigmoid_val = 1.0 / (1.0 + jnp.exp(-pre_act))
    return pre_act * sigmoid_val, sigmoid_val * (1.0 + pre_act * (1.0 - sigmoid_val))


def relay_kernel(
    parts,
    sections,
    tok_ref,
    cot_ref,
    gain_ref,
    wi_ref,
    wo_ref,
    cos_ref,
    sin_ref,
    par_ref,
    spec_ref,
    out_ref,
    gin_ref,
    res_ref,
    xbuf,
    gbuf,
    gate_act,
    gate_slope,
    val_slope,
    send_a,
    chan_a,
    zbuf,
    mix_chan,
    mix_tok,
    send_b,
    chan_b,
    dval_chan,
    dval_tok,
    dgate_send,
    dgate_chan,
    arr_chan,
    slope_chan,
    normed_all,
    gated_all,
    res_send,
    wo_t,
    wi_t,
    dnormed_gate,
    a2a_send,
    a2a_recv,
    own_sem,
    gat_send,
    gat_recv,
    fwd_send,
    fwd_recv,
    hop_send,
    hop_recv,
):
    f32, bf16 = jnp.float32, jnp.bfloat16
    sec = lax.axis_index("section")
    me = lax.axis_index("seq")
    rows, width = tok_ref.shape
    length = rows * parts
    cols = width // parts
    splits = hop_send.shape[1]
    bands = [slice(i * rows // splits, (i + 1) * rows // splits) for i in range(splits)]

    def ds(index, size):
        return pl.ds(pl.multiple_of(index * size, size), size)

    def peer(step):
        return lax.rem(me + step, parts)

    barrier = pltpu.get_barrier_semaphore()
    for step in range(1, parts):
        pl.semaphore_signal(barrier, inc=1, device_id={"seq": peer(step)})

    for step in (1, sections - 1):
        pl.semaphore_signal(
            barrier, inc=1, device_id={"section": lax.rem(sec + step, sections)}
        )
    pl.semaphore_wait(barrier, parts + 1)

    def exchange(slot, source, target):
        copies = []
        for step in range(1, parts):
            copies.append(
                pltpu.make_async_remote_copy(
                    src_ref=source(peer(step)),
                    dst_ref=target(me),
                    send_sem=a2a_send.at[slot, step],
                    recv_sem=a2a_recv.at[slot, step],
                    device_id={"seq": peer(step)},
                )
            )
        copies.append(pltpu.make_async_copy(source(me), target(me), own_sem.at[slot]))
        return copies

    def start(copies):
        for copy in copies:
            copy.start()

    def arrive(copies):
        for copy in copies[:-1]:
            copy.wait_recv()
        copies[-1].wait()

    def left(copies):
        for copy in copies[:-1]:
            copy.wait_send()

    def col_block(ref):
        return lambda device: ref.at[:, ds(device, cols)]

    def row_block(ref, size):
        return lambda device: ref.at[ds(device, size), :]

    def mix(source, target, sign):
        half = spec_ref.shape[1]
        chunk = min(half, 256)
        signal = source[...]
        nyquist = jnp.dot(par_ref[...], signal, preferred_element_type=f32)[:1, :]
        for first in range(0, half, chunk):
            band = slice(first, first + chunk)
            real = jnp.dot(cos_ref[band, :], signal, preferred_element_type=f32)
            imag = jnp.dot(sin_ref[band, :], signal, preferred_element_type=f32)
            if first == 0:
                lead = lax.broadcasted_iota(jnp.int32, imag.shape, 0) == 0
                imag = jnp.where(lead, nyquist, imag)
            k_re, k_im, k_ny = spec_ref[0, band, :], spec_ref[1, band, :], spec_ref[2, band, :]
            zbuf[band, :] = (real * k_re - sign * (imag * k_im)).astype(bf16)
            zbuf[half + first : half + first + chunk, :] = (
                sign * (real * k_im) + imag * k_ny
            ).astype(bf16)
        z_re, z_im = zbuf[:half, :], zbuf[half:, :]
        z_ny = zbuf[half : half + 1, :].astype(f32)
        for first in range(0, length, chunk):
            band = slice(first, first + chunk)
            total = jnp.dot(cos_ref[band, :], z_re, preferred_element_type=f32)
            total += jnp.dot(sin_ref[band, :], z_im, preferred_element_type=f32)
            odd = lax.broadcasted_iota(jnp.int32, total.shape, 0) % 2 == 1
            target[band, :] = (total + jnp.where(odd, -z_ny, z_ny)).astype(bf16)

    def hop(direction, ref, landing, to_section):
        return [
            pltpu.make_async_remote_copy(
                src_ref=ref.at[band, :],
                dst_ref=landing.at[band, :],
                send_sem=hop_send.at[direction, index],
                recv_sem=hop_recv.at[direction, index],
                device_id={"section": to_section},
            )
            for index, band in enumerate(bands)
        ]

    hop_fwd = hop(0, out_ref, xbuf, jnp.minimum(sec + 1, sections - 1))
    hop_bwd = hop(1, gin_ref, gbuf, jnp.maximum(sec - 1, 0))

    def transpose_weights():
        for first in range(0, width, 256):
            band = slice(first, first + 256)
            wo_t[:, band] = wo_ref[band, :].T
            wi_t[:, band] = wi_ref[band, :].T

    @pl.when(sec == 0)
    def _():
        xbuf[...] = tok_ref[...]

    @pl.when(sec > 0)
    def _():
        transpose_weights()

    gain = gain_ref[...]

    def scaled(band):
        x_float = xbuf[band, :].astype(f32)
        inv_rms = lax.rsqrt(jnp.mean(x_float * x_float, axis=1, keepdims=True) + EPSILON)
        return x_float * inv_rms, inv_rms

    def own(band):
        size = band.stop - band.start
        return pl.ds(pl.multiple_of(me * rows + band.start, size), size)

    def cols_at(ref, band):
        return lambda device: ref.at[band, ds(device, cols)]

    def rows_at(ref, band):
        size = band.stop - band.start
        return lambda device: ref.at[
            pl.ds(pl.multiple_of(device * rows + band.start, size), size), :
        ]

    to_chan, to_tok, grad_chan, grad_tok = [], [], [], []
    for index, band in enumerate(bands):
        to_chan.append(exchange(index, cols_at(send_a, band), rows_at(chan_a, band)))
        to_tok.append(exchange(splits + index, rows_at(mix_chan, band), cols_at(mix_tok, band)))
        grad_chan.append(
            exchange(2 * splits + index, cols_at(send_b, band), rows_at(chan_b, band))
        )
        grad_tok.append(
            exchange(3 * splits + index, rows_at(dval_chan, band), cols_at(dval_tok, band))
        )
    extra = 4 * splits
    slope_move = exchange(extra, col_block(val_slope), row_block(slope_chan, rows))
    arr_move = exchange(extra + 1, col_block(gbuf), row_block(arr_chan, rows))
    dgate_move = exchange(extra + 2, col_block(dgate_send), row_block(dgate_chan, rows))

    for index, band in enumerate(bands):

        @pl.when(sec > 0)
        def _():
            hop_fwd[index].wait_recv()

        x_hat, _ = scaled(band)
        normed = (x_hat * gain).astype(bf16)
        normed_all[own(band), :] = normed
        pre_val = jnp.dot(normed, wi_ref[:, width:], preferred_element_type=f32)
        act, slope = silu_pair(pre_val)
        send_a[band, :] = act.astype(bf16)
        start(to_chan[index])
        val_slope[band, :] = slope.astype(bf16)
    own_rows = ds(me, rows)
    pre_gate = jnp.dot(normed_all[own_rows, :], wi_ref[:, :width], preferred_element_type=f32)
    act, slope = silu_pair(pre_gate)
    gate_act[...] = act.astype(bf16)
    gate_slope[...] = slope
    for move in to_chan:
        arrive(move)
    mix(chan_a, mix_chan, 1.0)
    for move in to_tok:
        start(move)
    for index, band in enumerate(bands):
        arrive(to_tok[index])
        gated = (gate_act[band, :].astype(f32) * mix_tok[band, :].astype(f32)).astype(bf16)
        gated_all[own(band), :] = gated
        update = jnp.dot(gated, wo_ref[...], preferred_element_type=f32)
        out_ref[band, :] = (xbuf[band, :].astype(f32) + update).astype(bf16)

        @pl.when(sec < sections - 1)
        def _():
            hop_fwd[index].start()

    for move in to_chan + to_tok:
        left(move)

    partner = me + 1 - 2 * lax.rem(me, 2)
    chips = parts // 2
    far, near = [], []
    for index, ref in enumerate((normed_all, gated_all)):
        for step in range(chips):
            owner = lax.rem(me + parts - 2 * step, parts)
            if step > 0:
                far.append(
                    pltpu.make_async_remote_copy(
                        src_ref=ref.at[own_rows, :],
                        dst_ref=ref.at[own_rows, :],
                        send_sem=gat_send.at[index, step],
                        recv_sem=gat_recv.at[index, step],
                        device_id={"seq": peer(2 * step)},
                    )
                )
            near.append(
                pltpu.make_async_remote_copy(
                    src_ref=ref.at[ds(owner, rows), :],
                    dst_ref=ref.at[ds(owner, rows), :],
                    send_sem=fwd_send.at[index, step],
                    recv_sem=fwd_recv.at[index, step],
                    device_id={"seq": partner},
                )
            )

    def gather_start():
        start(slope_move)
        start(far)

    def gather_finish():
        for index in range(2):
            near[index * chips].start()
            for step in range(1, chips):
                far[index * (chips - 1) + step - 1].wait_recv()
                near[index * chips + step].start()
        for copy in near:
            copy.wait()
        for copy in far:
            copy.wait_send()
        arrive(slope_move)
        left(slope_move)

    early = sections // 2

    @pl.when(sec < sections - 1)
    def _():
        gather_start()

    @pl.when(sec == 0)
    def _():
        transpose_weights()

    @pl.when(sec < early)
    def _():
        gather_finish()

    @pl.when(sec == sections - 1)
    def _():
        gbuf[...] = cot_ref[...]

    for index, band in enumerate(bands):

        @pl.when(sec < sections - 1)
        def _():
            hop_bwd[index].wait_recv()

        dgated = jnp.dot(gbuf[band, :], wo_t[...], preferred_element_type=f32)
        send_b[band, :] = (dgated * gate_act[band, :].astype(f32)).astype(bf16)
        start(grad_chan[index])
        dgate_send[band, :] = (dgated * mix_tok[band, :].astype(f32) * gate_slope[band, :]).astype(
            bf16
        )
    dnormed_gate[...] = jnp.dot(dgate_send[...], wi_t[:width, :], preferred_element_type=f32)
    for move in grad_chan:
        arrive(move)
    mix(chan_b, dval_chan, -1.0)
    for move in grad_tok:
        start(move)

    def result(part, lhs, rhs):
        piece = lax.dot_general(
            lhs, rhs[...], (((0,), (0,)), ((), ())), preferred_element_type=f32
        )
        res_send[part] = piece.astype(bf16)

    for index, band in enumerate(bands):
        arrive(grad_tok[index])
        dpre_val = (dval_tok[band, :].astype(f32) * val_slope[band, :].astype(f32)).astype(bf16)
        dnormed = dnormed_gate[band, :] + jnp.dot(
            dpre_val, wi_t[width:, :], preferred_element_type=f32
        )
        dscaled = dnormed * gain
        x_hat, inv_rms = scaled(band)
        shared = jnp.mean(dscaled * x_hat, axis=1, keepdims=True)
        gin_ref[band, :] = (
            gbuf[band, :].astype(f32) + inv_rms * (dscaled - x_hat * shared)
        ).astype(bf16)

        @pl.when(sec > 0)
        def _():
            hop_bwd[index].start()

    start(arr_move)
    start(dgate_move)

    @pl.when(sec == sections - 1)
    def _():
        gather_start()

    @pl.when(sec >= early)
    def _():
        gather_finish()

    moves = []
    for part in range(3):
        if part == 0:
            dval = (dval_chan[...].astype(f32) * slope_chan[...].astype(f32)).astype(bf16)
            result(0, dval, normed_all)
        elif part == 1:
            arrive(arr_move)
            result(1, arr_chan[...], gated_all)
        else:
            arrive(dgate_move)
            result(2, dgate_chan[...], normed_all)
        move = exchange(
            extra + 3 + part,
            lambda device, part=part: res_send.at[part, :, ds(device, cols)],
            lambda device, part=part: res_ref.at[part, ds(device, cols), :],
        )
        start(move)
        moves.append(move)
    for move in moves:
        arrive(move)
        left(move)
    for move in grad_chan + grad_tok + [arr_move, dgate_move]:
        left(move)

    for index in range(splits):

        @pl.when(sec < sections - 1)
        def _():
            hop_fwd[index].wait_send()

        @pl.when(sec > 0)
        def _():
            hop_bwd[index].wait_send()


def on_device(
    tokens, cotangent, norm_gain, w_inner, w_outer, rpe_periods, rpe_in, rpe_mid, rpe_out, decay
):
    rows, width = tokens.shape
    parts = lax.axis_size("seq")
    sections = lax.axis_size("section")
    cols = width // parts
    length = rows * parts
    if cols % 128 or rows % 128 or length > 1024 or parts % 2 or sections < 2:
        return on_device_factored(
            tokens, cotangent, norm_gain, w_inner, w_outer, rpe_periods, rpe_in, rpe_mid, rpe_out, decay
        )
    bf16, f32 = jnp.bfloat16, jnp.float32
    splits = SPLITS
    cos, sin, parity = dense_tables(length)
    kernel = kernel_rows(rpe_periods[0], rpe_in[0], rpe_mid[0], rpe_out[0], decay[0], length)
    kernel = kernel.T.astype(bf16)
    real, imag, nyquist = (
        jnp.dot(table, kernel, preferred_element_type=f32) for table in (cos, sin, parity)
    )
    first = lax.broadcasted_iota(jnp.int32, (length, 1), 0) == 0
    scale = jnp.where(first, 0.5, 1.0) / length
    spec = jnp.stack([real, imag, jnp.where(first, nyquist[:1], real)]) * scale
    tok_block = lambda kind: pltpu.VMEM((rows, width), kind)
    chan_block = lambda kind: pltpu.VMEM((length, cols), kind)
    vmem = pl.BlockSpec(memory_space=pltpu.VMEM)
    dma = pltpu.SemaphoreType.DMA
    out, grad_in, res = pl.pallas_call(
        functools.partial(relay_kernel, parts, sections),
        out_shape=(
            jax.ShapeDtypeStruct((rows, width), bf16),
            jax.ShapeDtypeStruct((rows, width), bf16),
            jax.ShapeDtypeStruct((3, width, cols), bf16),
        ),
        in_specs=[vmem] * 9,
        out_specs=(vmem,) * 3,
        scratch_shapes=[
            tok_block(bf16),
            tok_block(bf16),
            tok_block(bf16),
            tok_block(f32),
            tok_block(bf16),
            tok_block(bf16),
            chan_block(bf16),
            pltpu.VMEM((2 * length, cols), bf16),
            chan_block(bf16),
            tok_block(bf16),
            tok_block(bf16),
            chan_block(bf16),
            chan_block(bf16),
            tok_block(bf16),
            tok_block(bf16),
            chan_block(bf16),
            chan_block(bf16),
            chan_block(bf16),
            pltpu.VMEM((length, width), bf16),
            pltpu.VMEM((length, width), bf16),
            pltpu.VMEM((3, cols, width), bf16),
            pltpu.VMEM((width, width), bf16),
            pltpu.VMEM((2 * width, width), bf16),
            tok_block(f32),
            dma((4 * splits + 6, parts)),
            dma((4 * splits + 6, parts)),
            dma((4 * splits + 6,)),
            dma((2, parts // 2)),
            dma((2, parts // 2)),
            dma((2, parts // 2)),
            dma((2, parts // 2)),
            dma((2, splits)),
            dma((2, splits)),
        ],
        compiler_params=pltpu.CompilerParams(
            collective_id=0, has_side_effects=True, vmem_limit_bytes=60 * 1024 * 1024
        ),
    )(
        tokens,
        cotangent,
        norm_gain,
        w_inner[0],
        w_outer[0],
        cos,
        sin,
        parity,
        spec,
    )
    grad_scale = 1.0 / math.sqrt(length)
    inner = jnp.concatenate([res[2], res[0]], axis=0).T.astype(f32) * grad_scale
    outer = res[1].T.astype(f32) * grad_scale
    return (out[None], grad_in[None], inner[None], outer[None])


def solution(mesh):
    return jax.shard_map(
        on_device,
        mesh=mesh,
        in_specs=(
            P("seq", None),
            P("seq", None),
            P("section", None),
            P("section", None, None),
            P("section", None, None),
            P("section", None),
            P("section", None, None),
            P("section", None, None),
            P("section", None, "seq"),
            P("section", "seq"),
        ),
        out_specs=(
            P("section", "seq", None),
            P("section", "seq", None),
            P("section", "seq", None),
            P("section", "seq", None),
        ),
        check_vma=False,
    )
```

```python
import functools
import math

import jax
import jax.numpy as jnp
import numpy as np
from jax import lax
from jax.experimental import pallas as pl
from jax.experimental.pallas import tpu as pltpu
from jax.sharding import PartitionSpec as P

EPSILON = 1e-06
PRECISE = lax.Precision.HIGHEST


def passed_along(value, axis, steps):
    count = lax.axis_size(axis)
    initial, last = (max(0, -steps), min(count, count - steps))
    return lax.ppermute(value, axis, [(source, source + steps) for source in range(initial, last)])


def kernel_rows(periods, weight_in, weight_mid, weight_out, decay_rate, seq_length, precise=PRECISE):
    positions = jnp.arange(seq_length, dtype=jnp.int32)
    turn_count = periods[:, None] * positions[None, :] % seq_length
    angles = turn_count.astype(jnp.float32) * (2.0 * math.pi / seq_length)
    features = jnp.concatenate([jnp.sin(angles), jnp.cos(angles)], axis=0)
    hidden = jax.nn.relu(jnp.dot(weight_in.T, features, precision=precise))
    hidden = jax.nn.relu(jnp.dot(weight_mid.T, hidden, precision=precise))
    raw_rows = jnp.dot(weight_out.T, hidden, precision=precise)
    place = positions.astype(jnp.float32)
    norm_scale = jnp.sqrt(1.0 - jnp.exp(-2.0 * decay_rate))
    return raw_rows * norm_scale[:, None] * jnp.exp(-decay_rate[:, None] * place[None, :])


def silu_slope(pre_act):
    sigmoid_val = jax.nn.sigmoid(pre_act)
    return sigmoid_val * (1.0 + pre_act * (1.0 - sigmoid_val))


def split_size(fft_size):
    return math.gcd(fft_size, 1 << (fft_size.bit_length() - 1) // 2)


def dft_table(length, sign_value):
    indices = jnp.arange(length, dtype=jnp.int32)
    turn_count = indices[:, None] * indices[None, :] % length
    angles = turn_count.astype(jnp.float32) * (sign_value * 2.0 * math.pi / length)
    return (jnp.cos(angles), jnp.sin(angles))


def twiddle_table(count_rows, count_cols, sign_value):
    fft_size = count_rows * count_cols
    turn_count = (
        jnp.arange(count_rows, dtype=jnp.int32)[:, None]
        * jnp.arange(count_cols, dtype=jnp.int32)[None, :]
    )
    angles = turn_count.astype(jnp.float32) * (sign_value * 2.0 * math.pi / fft_size)
    return (jnp.cos(angles), jnp.sin(angles))


def half_table(size_second):
    half_cols = size_second // 2
    turn_count = (
        jnp.arange(half_cols, dtype=jnp.int32)[:, None]
        * jnp.arange(size_second, dtype=jnp.int32)[None, :]
        % size_second
    )
    angles = turn_count.astype(jnp.float32) * (2.0 * math.pi / size_second)
    return (jnp.cos(angles), jnp.sin(angles))


def parity_signs(size_second):
    return 1.0 - 2.0 * (jnp.arange(size_second, dtype=jnp.int32) % 2).astype(jnp.float32)


def spectrum(signal, size_first):
    own_chans, seq_length = signal.shape
    fft_size = 2 * seq_length
    size_second = fft_size // size_first
    half_rows = size_first // 2
    shaped = signal.reshape(own_chans, half_rows, size_second)
    first_re, first_im = dft_table(size_first, -1.0)
    first_both = jnp.concatenate([first_re[:, :half_rows], first_im[:, :half_rows]], axis=0)
    section = jnp.einsum("kp,cpq->ckq", first_both, shaped, precision=PRECISE)
    section_re = section[:, :size_first]
    section_im = section[:, size_first:]
    twist_re, twist_im = twiddle_table(size_first, size_second, -1.0)
    turned = jnp.concatenate(
        [
            section_re * twist_re - section_im * twist_im,
            section_re * twist_im + section_im * twist_re,
        ],
        axis=2,
    )
    cos_rows, sin_rows = half_table(size_second)
    cos_cols = cos_rows.T
    sin_cols = sin_rows.T
    second_both = jnp.concatenate(
        [
            jnp.concatenate([cos_cols, -sin_cols], axis=1),
            jnp.concatenate([sin_cols, cos_cols], axis=1),
        ],
        axis=0,
    )
    spec = jnp.einsum("ckq,qm->ckm", turned, second_both, precision=PRECISE)
    nyquist = jnp.einsum("cpq,q->c", shaped, parity_signs(size_second), precision=PRECISE)
    return (spec, nyquist[:, None])


def to_signal(spec, nyquist, size_first):
    own_chans, _, size_second = spec.shape
    half_cols = size_second // 2
    half_rows = size_first // 2
    fft_size = size_first * size_second
    row_ids = jnp.arange(size_first, dtype=jnp.int32)[:, None]
    col_ids = jnp.arange(half_cols, dtype=jnp.int32)[None, :]
    weights = jnp.where((row_ids == 0) & (col_ids == 0), 1.0, 2.0).astype(jnp.float32)
    weighted = spec * jnp.concatenate([weights, weights], axis=1)
    cos_rows, sin_rows = half_table(size_second)
    inner_both = jnp.concatenate(
        [
            jnp.concatenate([cos_rows, sin_rows], axis=1),
            jnp.concatenate([-sin_rows, cos_rows], axis=1),
        ],
        axis=0,
    )
    section = jnp.einsum("ckm,mq->ckq", weighted, inner_both, precision=PRECISE)
    section_re = section[:, :, :size_second]
    section_im = section[:, :, size_second:]
    twist_re, twist_im = twiddle_table(size_first, size_second, 1.0)
    turned = jnp.concatenate(
        [
            section_re * twist_re - section_im * twist_im,
            section_re * twist_im + section_im * twist_re,
        ],
        axis=1,
    )
    first_re, first_im = dft_table(size_first, 1.0)
    outer_both = jnp.concatenate([first_re[:half_rows], -first_im[:half_rows]], axis=1)
    signal = jnp.einsum("pk,ckq->cpq", outer_both, turned, precision=PRECISE)
    signal = signal + nyquist[:, :, None] * parity_signs(size_second)[None, None, :]
    return (signal / fft_size).reshape(own_chans, half_rows * size_second)


def on_device_factored(
    tokens, cotangent, norm_gain, w_inner, w_outer, rpe_periods, rpe_in, rpe_mid, rpe_out, decay
):
    tok_rows, model_width = tokens.shape
    seq_parts = lax.axis_size("seq")
    seq_length = tok_rows * seq_parts
    own_chans = model_width // seq_parts
    fft_size = 2 * seq_length
    size_first = split_size(fft_size)
    half_cols = fft_size // size_first // 2
    section_index = lax.axis_index("section")
    section_count = lax.axis_size("section")
    grad_scale = 1.0 / math.sqrt(seq_length)
    gain_row = norm_gain[0]
    inner_weight = w_inner[0]
    outer_weight = w_outer[0]

    def to_channels(block):
        return lax.all_to_all(block, "seq", split_axis=0, concat_axis=1, tiled=True)

    def to_tokens(block):
        return lax.all_to_all(block, "seq", split_axis=1, concat_axis=0, tiled=True)

    def pass_section(block, offset):
        return passed_along(block, "section", offset)

    def token_front(inputs):
        x_float = inputs.astype(jnp.float32)
        inv_rms = lax.rsqrt(jnp.mean(x_float * x_float, axis=1, keepdims=True) + EPSILON)
        normed = (x_float * inv_rms * gain_row[None, :]).astype(jnp.bfloat16)
        pre_act = jnp.einsum("td,de->et", normed, inner_weight, preferred_element_type=jnp.float32)
        value_act = jax.nn.silu(pre_act[model_width:]).astype(jnp.bfloat16)
        return (inv_rms, normed, pre_act, value_act)

    kernel = kernel_rows(rpe_periods[0], rpe_in[0], rpe_mid[0], rpe_out[0], decay[0], seq_length)
    forward_spec, forward_nyq = spectrum(kernel, size_first)

    def channel_forward(value_chan):
        value_spec, value_nyq = spectrum(value_chan.astype(jnp.float32), size_first)
        kernel_re = forward_spec[:, :, :half_cols]
        kernel_im = forward_spec[:, :, half_cols:]
        value_re = value_spec[:, :, :half_cols]
        value_im = value_spec[:, :, half_cols:]
        product = jnp.concatenate(
            [
                value_re * kernel_re - value_im * kernel_im,
                value_re * kernel_im + value_im * kernel_re,
            ],
            axis=2,
        )
        mixed_chan = to_signal(product, value_nyq * forward_nyq, size_first)
        return mixed_chan.astype(jnp.bfloat16)

    def token_back(inputs, pre_act, mixed_tok):
        gate_act = jax.nn.silu(pre_act[:model_width]).astype(jnp.bfloat16)
        gated = (gate_act.astype(jnp.float32) * mixed_tok.astype(jnp.float32)).astype(jnp.bfloat16)
        update = jnp.einsum("et,ef->tf", gated, outer_weight, preferred_element_type=jnp.float32)
        return (gated, (inputs.astype(jnp.float32) + update).astype(jnp.bfloat16))

    zero_tok = jnp.zeros((tok_rows, model_width), jnp.bfloat16)
    zero_cols = jnp.zeros((model_width, tok_rows), jnp.bfloat16)
    zero_chan = jnp.zeros((own_chans, seq_length), jnp.bfloat16)
    current = tokens
    kept_input = zero_tok
    kept_front = (
        jnp.zeros((tok_rows, 1), jnp.float32),
        zero_tok,
        jnp.zeros((2 * model_width, tok_rows), jnp.float32),
        zero_cols,
    )
    kept_mixed = zero_cols
    kept_gated = zero_cols
    produced = zero_tok
    for section_step in range(section_count):
        active = section_index == section_step
        source = current
        kept_input = jnp.where(active, source, kept_input)
        kept_front = lax.cond(
            active, lambda: token_front(source), lambda previous=kept_front: previous
        )
        value_chan = to_channels(kept_front[3])
        mixed_chan = lax.cond(active, lambda: channel_forward(value_chan), lambda: zero_chan)
        mixed_tok = to_tokens(mixed_chan)
        kept_mixed = jnp.where(active, mixed_tok, kept_mixed)
        front_now = kept_front
        kept_gated, produced = lax.cond(
            active,
            lambda: token_back(source, front_now[2], mixed_tok),
            lambda previous=(kept_gated, produced): previous,
        )
        if section_step + 1 < section_count:
            current = pass_section(produced, 1)
    inv_rms, normed, pre_act, value_act = kept_front
    backward_spec, backward_nyq = (forward_spec, forward_nyq)

    def grad_front(grad_out):
        dgated = jnp.einsum("tf,ef->et", grad_out, outer_weight, preferred_element_type=jnp.float32)
        gate_act = jax.nn.silu(pre_act[:model_width]).astype(jnp.bfloat16)
        dmixed = (dgated * gate_act.astype(jnp.float32)).astype(jnp.bfloat16)
        return (dmixed, dgated * kept_mixed.astype(jnp.float32))

    def channel_backward(dmixed_chan):
        kernel_re = backward_spec[:, :, :half_cols]
        kernel_im = backward_spec[:, :, half_cols:]
        grad_spec, grad_nyq = spectrum(dmixed_chan.astype(jnp.float32), size_first)
        grad_re = grad_spec[:, :, :half_cols]
        grad_im = grad_spec[:, :, half_cols:]
        product = jnp.concatenate(
            [grad_re * kernel_re + grad_im * kernel_im, grad_im * kernel_re - grad_re * kernel_im],
            axis=2,
        )
        dvalue_chan = to_signal(product, grad_nyq * backward_nyq, size_first)
        return dvalue_chan.astype(jnp.bfloat16)

    def grad_back(dvalue_tok, dgate, grad_out):
        dpre = jnp.concatenate(
            [
                dgate * silu_slope(pre_act[:model_width]),
                dvalue_tok.astype(jnp.float32) * silu_slope(pre_act[model_width:]),
            ],
            axis=0,
        ).astype(jnp.bfloat16)
        dnormed = jnp.einsum("et,de->td", dpre, inner_weight, preferred_element_type=jnp.float32)
        x_float = kept_input.astype(jnp.float32)
        dscaled = dnormed * gain_row[None, :]
        x_hat = x_float * inv_rms
        shared = jnp.mean(dscaled * x_hat, axis=1, keepdims=True)
        grad_in = (grad_out.astype(jnp.float32) + inv_rms * (dscaled - x_hat * shared)).astype(
            jnp.bfloat16
        )
        return (dpre, grad_in)

    grad_now = cotangent
    grad_input = zero_tok
    kept_grad = zero_tok
    kept_dgate = jnp.zeros((model_width, tok_rows), jnp.float32)
    kept_dpre = jnp.zeros((2 * model_width, tok_rows), jnp.bfloat16)
    for section_step in reversed(range(section_count)):
        active = section_index == section_step
        arriving = grad_now
        kept_grad = jnp.where(active, arriving, kept_grad)
        dmixed_tok, kept_dgate = lax.cond(
            active, lambda: grad_front(arriving), lambda previous=kept_dgate: (zero_cols, previous)
        )
        dmixed_chan = to_channels(dmixed_tok)
        dvalue_chan = lax.cond(active, lambda: channel_backward(dmixed_chan), lambda: zero_chan)
        dvalue_tok = to_tokens(dvalue_chan)
        dgate_now = kept_dgate
        kept_dpre, grad_input = lax.cond(
            active,
            lambda: grad_back(dvalue_tok, dgate_now, arriving),
            lambda previous=(kept_dpre, grad_input): previous,
        )
        if section_step > 0:
            grad_now = pass_section(grad_input, -1)
    inner_term = jnp.einsum("tr,et->re", normed, kept_dpre, preferred_element_type=jnp.float32)
    outer_term = jnp.einsum("et,tf->ef", kept_gated, kept_grad, preferred_element_type=jnp.float32)
    inner_sum, outer_sum = (
        lax.psum_scatter(inner_term, "seq", scatter_dimension=0, tiled=True),
        lax.psum_scatter(outer_term, "seq", scatter_dimension=0, tiled=True),
    )
    return (
        produced[None],
        grad_input[None],
        (inner_sum * grad_scale)[None],
        (outer_sum * grad_scale)[None],
    )


SPLITS = 4


def dense_tables(seq_length):
    fft_size = 2 * seq_length
    coarse = math.gcd(seq_length, 32)
    fine = seq_length // coarse
    place = np.arange(seq_length, dtype=np.int64)

    def pair(freqs):
        angles = 2.0 * np.pi / fft_size * (freqs[:, None] * place[None, :] % fft_size)
        return (np.cos(angles).astype(np.float32), np.sin(angles).astype(np.float32))

    high_cos, high_sin = pair(np.arange(coarse, dtype=np.int64) * fine)
    low_cos, low_sin = pair(np.arange(fine, dtype=np.int64))
    parity = np.broadcast_to((1.0 - 2.0 * (place % 2)).astype(np.float32), (16, seq_length))
    shape = (seq_length, seq_length)
    hc, hs = jnp.asarray(high_cos)[:, None, :], jnp.asarray(high_sin)[:, None, :]
    lc, ls = jnp.asarray(low_cos)[None], jnp.asarray(low_sin)[None]
    cos = (hc * lc - hs * ls).reshape(shape).astype(jnp.bfloat16)
    sin = (-(hs * lc + hc * ls)).reshape(shape).astype(jnp.bfloat16)
    return cos, sin, jnp.asarray(parity).astype(jnp.bfloat16)


def silu_pair(pre_act):
    sigmoid_val = 1.0 / (1.0 + jnp.exp(-pre_act))
    return pre_act * sigmoid_val, sigmoid_val * (1.0 + pre_act * (1.0 - sigmoid_val))


def relay_kernel(
    parts,
    sections,
    tok_ref,
    cot_ref,
    gain_ref,
    wi_ref,
    wo_ref,
    cos_ref,
    sin_ref,
    par_ref,
    spec_ref,
    out_ref,
    gin_ref,
    res_ref,
    xbuf,
    gbuf,
    gate_act,
    gate_slope,
    val_slope,
    send_a,
    chan_a,
    zbuf,
    mix_chan,
    mix_tok,
    send_b,
    chan_b,
    dval_chan,
    dval_tok,
    dgate_send,
    dgate_chan,
    arr_chan,
    slope_chan,
    normed_all,
    gated_all,
    res_send,
    wo_t,
    wi_t,
    dnormed_gate,
    a2a_send,
    a2a_recv,
    own_sem,
    gat_send,
    gat_recv,
    fwd_send,
    fwd_recv,
    hop_send,
    hop_recv,
):
    f32, bf16 = jnp.float32, jnp.bfloat16
    sec = lax.axis_index("section")
    me = lax.axis_index("seq")
    rows, width = tok_ref.shape
    length = rows * parts
    cols = width // parts
    splits = hop_send.shape[1]
    bands = [slice(i * rows // splits, (i + 1) * rows // splits) for i in range(splits)]

    def ds(index, size):
        return pl.ds(pl.multiple_of(index * size, size), size)

    def peer(step):
        return lax.rem(me + step, parts)

    barrier = pltpu.get_barrier_semaphore()
    for step in range(1, parts):
        pl.semaphore_signal(barrier, inc=1, device_id={"seq": peer(step)})

    for step in (1, sections - 1):
        pl.semaphore_signal(
            barrier, inc=1, device_id={"section": lax.rem(sec + step, sections)}
        )
    pl.semaphore_wait(barrier, parts + 1)

    def exchange(slot, source, target):
        copies = []
        for step in range(1, parts):
            copies.append(
                pltpu.make_async_remote_copy(
                    src_ref=source(peer(step)),
                    dst_ref=target(me),
                    send_sem=a2a_send.at[slot, step],
                    recv_sem=a2a_recv.at[slot, step],
                    device_id={"seq": peer(step)},
                )
            )
        copies.append(pltpu.make_async_copy(source(me), target(me), own_sem.at[slot]))
        return copies

    def start(copies):
        for copy in copies:
            copy.start()

    def arrive(copies):
        for copy in copies[:-1]:
            copy.wait_recv()
        copies[-1].wait()

    def left(copies):
        for copy in copies[:-1]:
            copy.wait_send()

    def col_block(ref):
        return lambda device: ref.at[:, ds(device, cols)]

    def row_block(ref, size):
        return lambda device: ref.at[ds(device, size), :]

    def mix(source, target, sign):
        half = spec_ref.shape[1]
        chunk = min(half, 256)
        signal = source[...]
        nyquist = jnp.dot(par_ref[...], signal, preferred_element_type=f32)[:1, :]
        for first in range(0, half, chunk):
            band = slice(first, first + chunk)
            real = jnp.dot(cos_ref[band, :], signal, preferred_element_type=f32)
            imag = jnp.dot(sin_ref[band, :], signal, preferred_element_type=f32)
            if first == 0:
                lead = lax.broadcasted_iota(jnp.int32, imag.shape, 0) == 0
                imag = jnp.where(lead, nyquist, imag)
            k_re, k_im, k_ny = spec_ref[0, band, :], spec_ref[1, band, :], spec_ref[2, band, :]
            zbuf[band, :] = (real * k_re - sign * (imag * k_im)).astype(bf16)
            zbuf[half + first : half + first + chunk, :] = (
                sign * (real * k_im) + imag * k_ny
            ).astype(bf16)
        z_re, z_im = zbuf[:half, :], zbuf[half:, :]
        z_ny = zbuf[half : half + 1, :].astype(f32)
        for first in range(0, length, chunk):
            band = slice(first, first + chunk)
            total = jnp.dot(cos_ref[band, :], z_re, preferred_element_type=f32)
            total += jnp.dot(sin_ref[band, :], z_im, preferred_element_type=f32)
            odd = lax.broadcasted_iota(jnp.int32, total.shape, 0) % 2 == 1
            target[band, :] = (total + jnp.where(odd, -z_ny, z_ny)).astype(bf16)

    def hop(direction, ref, landing, to_section):
        return [
            pltpu.make_async_remote_copy(
                src_ref=ref.at[band, :],
                dst_ref=landing.at[band, :],
                send_sem=hop_send.at[direction, index],
                recv_sem=hop_recv.at[direction, index],
                device_id={"section": to_section},
            )
            for index, band in enumerate(bands)
        ]

    hop_fwd = hop(0, out_ref, xbuf, jnp.minimum(sec + 1, sections - 1))
    hop_bwd = hop(1, gin_ref, gbuf, jnp.maximum(sec - 1, 0))

    def transpose_weights():
        for first in range(0, width, 256):
            band = slice(first, first + 256)
            wo_t[:, band] = wo_ref[band, :].T
            wi_t[:, band] = wi_ref[band, :].T

    @pl.when(sec == 0)
    def _():
        xbuf[...] = tok_ref[...]

    @pl.when(sec > 0)
    def _():
        transpose_weights()

    gain = gain_ref[...]

    def scaled(band):
        x_float = xbuf[band, :].astype(f32)
        inv_rms = lax.rsqrt(jnp.mean(x_float * x_float, axis=1, keepdims=True) + EPSILON)
        return x_float * inv_rms, inv_rms

    def own(band):
        size = band.stop - band.start
        return pl.ds(pl.multiple_of(me * rows + band.start, size), size)

    def cols_at(ref, band):
        return lambda device: ref.at[band, ds(device, cols)]

    def rows_at(ref, band):
        size = band.stop - band.start
        return lambda device: ref.at[
            pl.ds(pl.multiple_of(device * rows + band.start, size), size), :
        ]

    to_chan, to_tok, grad_chan, grad_tok = [], [], [], []
    for index, band in enumerate(bands):
        to_chan.append(exchange(index, cols_at(send_a, band), rows_at(chan_a, band)))
        to_tok.append(exchange(splits + index, rows_at(mix_chan, band), cols_at(mix_tok, band)))
        grad_chan.append(
            exchange(2 * splits + index, cols_at(send_b, band), rows_at(chan_b, band))
        )
        grad_tok.append(
            exchange(3 * splits + index, rows_at(dval_chan, band), cols_at(dval_tok, band))
        )
    extra = 4 * splits
    slope_move = exchange(extra, col_block(val_slope), row_block(slope_chan, rows))
    arr_move = exchange(extra + 1, col_block(gbuf), row_block(arr_chan, rows))
    dgate_move = exchange(extra + 2, col_block(dgate_send), row_block(dgate_chan, rows))

    for index, band in enumerate(bands):

        @pl.when(sec > 0)
        def _():
            hop_fwd[index].wait_recv()

        x_hat, _ = scaled(band)
        normed = (x_hat * gain).astype(bf16)
        normed_all[own(band), :] = normed
        pre_val = jnp.dot(normed, wi_ref[:, width:], preferred_element_type=f32)
        act, slope = silu_pair(pre_val)
        send_a[band, :] = act.astype(bf16)
        start(to_chan[index])
        val_slope[band, :] = slope.astype(bf16)
    own_rows = ds(me, rows)
    pre_gate = jnp.dot(normed_all[own_rows, :], wi_ref[:, :width], preferred_element_type=f32)
    act, slope = silu_pair(pre_gate)
    gate_act[...] = act.astype(bf16)
    gate_slope[...] = slope
    for move in to_chan:
        arrive(move)
    mix(chan_a, mix_chan, 1.0)
    for move in to_tok:
        start(move)
    for index, band in enumerate(bands):
        arrive(to_tok[index])
        gated = (gate_act[band, :].astype(f32) * mix_tok[band, :].astype(f32)).astype(bf16)
        gated_all[own(band), :] = gated
        update = jnp.dot(gated, wo_ref[...], preferred_element_type=f32)
        out_ref[band, :] = (xbuf[band, :].astype(f32) + update).astype(bf16)

        @pl.when(sec < sections - 1)
        def _():
            hop_fwd[index].start()

    for move in to_chan + to_tok:
        left(move)

    partner = me + 1 - 2 * lax.rem(me, 2)
    chips = parts // 2
    far, near = [], []
    for index, ref in enumerate((normed_all, gated_all)):
        for step in range(chips):
            owner = lax.rem(me + parts - 2 * step, parts)
            if step > 0:
                far.append(
                    pltpu.make_async_remote_copy(
                        src_ref=ref.at[own_rows, :],
                        dst_ref=ref.at[own_rows, :],
                        send_sem=gat_send.at[index, step],
                        recv_sem=gat_recv.at[index, step],
                        device_id={"seq": peer(2 * step)},
                    )
                )
            near.append(
                pltpu.make_async_remote_copy(
                    src_ref=ref.at[ds(owner, rows), :],
                    dst_ref=ref.at[ds(owner, rows), :],
                    send_sem=fwd_send.at[index, step],
                    recv_sem=fwd_recv.at[index, step],
                    device_id={"seq": partner},
                )
            )

    def gather_start():
        start(slope_move)
        start(far)

    def gather_finish():
        for index in range(2):
            near[index * chips].start()
            for step in range(1, chips):
                far[index * (chips - 1) + step - 1].wait_recv()
                near[index * chips + step].start()
        for copy in near:
            copy.wait()
        for copy in far:
            copy.wait_send()
        arrive(slope_move)
        left(slope_move)

    early = sections // 2

    @pl.when(sec < sections - 1)
    def _():
        gather_start()

    @pl.when(sec == 0)
    def _():
        transpose_weights()

    @pl.when(sec < early)
    def _():
        gather_finish()

    @pl.when(sec == sections - 1)
    def _():
        gbuf[...] = cot_ref[...]

    for index, band in enumerate(bands):

        @pl.when(sec < sections - 1)
        def _():
            hop_bwd[index].wait_recv()

        dgated = jnp.dot(gbuf[band, :], wo_t[...], preferred_element_type=f32)
        send_b[band, :] = (dgated * gate_act[band, :].astype(f32)).astype(bf16)
        start(grad_chan[index])
        dgate_send[band, :] = (dgated * mix_tok[band, :].astype(f32) * gate_slope[band, :]).astype(
            bf16
        )

    @pl.when(sec == 0)
    def _():
        start(arr_move)
        start(dgate_move)

    dnormed_gate[...] = jnp.dot(dgate_send[...], wi_t[:width, :], preferred_element_type=f32)
    for move in grad_chan:
        arrive(move)
    mix(chan_b, dval_chan, -1.0)
    for move in grad_tok:
        start(move)

    def result(part, lhs, rhs):
        piece = lax.dot_general(
            lhs, rhs[...], (((0,), (0,)), ((), ())), preferred_element_type=f32
        )
        res_send[part] = piece.astype(bf16)

    moves = [
        exchange(
            extra + 3 + part,
            lambda device, part=part: res_send.at[part, :, ds(device, cols)],
            lambda device, part=part: res_ref.at[part, ds(device, cols), :],
        )
        for part in range(3)
    ]

    def weight_grads():
        dval = (dval_chan[...].astype(f32) * slope_chan[...].astype(f32)).astype(bf16)
        result(0, dval, normed_all)
        start(moves[0])
        arrive(arr_move)
        result(1, arr_chan[...], gated_all)
        start(moves[1])
        arrive(dgate_move)
        result(2, dgate_chan[...], normed_all)
        start(moves[2])

    @pl.when(sec == 0)
    def _():
        weight_grads()

    for index, band in enumerate(bands):
        arrive(grad_tok[index])
        dpre_val = (dval_tok[band, :].astype(f32) * val_slope[band, :].astype(f32)).astype(bf16)
        dnormed = dnormed_gate[band, :] + jnp.dot(
            dpre_val, wi_t[width:, :], preferred_element_type=f32
        )
        dscaled = dnormed * gain
        x_hat, inv_rms = scaled(band)
        shared = jnp.mean(dscaled * x_hat, axis=1, keepdims=True)
        gin_ref[band, :] = (
            gbuf[band, :].astype(f32) + inv_rms * (dscaled - x_hat * shared)
        ).astype(bf16)

        @pl.when(sec > 0)
        def _():
            hop_bwd[index].start()

    @pl.when(sec > 0)
    def _():
        start(arr_move)
        start(dgate_move)

    @pl.when(sec == sections - 1)
    def _():
        gather_start()

    @pl.when(sec >= early)
    def _():
        gather_finish()

    @pl.when(sec > 0)
    def _():
        weight_grads()

    for move in moves:
        arrive(move)
        left(move)
    for move in grad_chan + grad_tok + [arr_move, dgate_move]:
        left(move)

    for index in range(splits):

        @pl.when(sec < sections - 1)
        def _():
            hop_fwd[index].wait_send()

        @pl.when(sec > 0)
        def _():
            hop_bwd[index].wait_send()


def on_device(
    tokens, cotangent, norm_gain, w_inner, w_outer, rpe_periods, rpe_in, rpe_mid, rpe_out, decay
):
    rows, width = tokens.shape
    parts = lax.axis_size("seq")
    sections = lax.axis_size("section")
    cols = width // parts
    length = rows * parts
    if cols % 128 or rows % 128 or length > 1024 or parts % 2 or sections < 2:
        return on_device_factored(
            tokens, cotangent, norm_gain, w_inner, w_outer, rpe_periods, rpe_in, rpe_mid, rpe_out, decay
        )
    bf16, f32 = jnp.bfloat16, jnp.float32
    splits = SPLITS
    cos, sin, parity = dense_tables(length)
    kernel = kernel_rows(rpe_periods[0], rpe_in[0], rpe_mid[0], rpe_out[0], decay[0], length, lax.Precision.HIGH)
    kernel = kernel.T.astype(bf16)
    real, imag, nyquist = (
        jnp.dot(table, kernel, preferred_element_type=f32) for table in (cos, sin, parity)
    )
    first = lax.broadcasted_iota(jnp.int32, (length, 1), 0) == 0
    scale = jnp.where(first, 0.5, 1.0) / length
    spec = jnp.stack([real, imag, jnp.where(first, nyquist[:1], real)]) * scale
    tok_block = lambda kind: pltpu.VMEM((rows, width), kind)
    chan_block = lambda kind: pltpu.VMEM((length, cols), kind)
    vmem = pl.BlockSpec(memory_space=pltpu.VMEM)
    dma = pltpu.SemaphoreType.DMA
    out, grad_in, res = pl.pallas_call(
        functools.partial(relay_kernel, parts, sections),
        out_shape=(
            jax.ShapeDtypeStruct((rows, width), bf16),
            jax.ShapeDtypeStruct((rows, width), bf16),
            jax.ShapeDtypeStruct((3, width, cols), bf16),
        ),
        in_specs=[vmem] * 9,
        out_specs=(vmem,) * 3,
        scratch_shapes=[
            tok_block(bf16),
            tok_block(bf16),
            tok_block(bf16),
            tok_block(f32),
            tok_block(bf16),
            tok_block(bf16),
            chan_block(bf16),
            pltpu.VMEM((2 * length, cols), bf16),
            chan_block(bf16),
            tok_block(bf16),
            tok_block(bf16),
            chan_block(bf16),
            chan_block(bf16),
            tok_block(bf16),
            tok_block(bf16),
            chan_block(bf16),
            chan_block(bf16),
            chan_block(bf16),
            pltpu.VMEM((length, width), bf16),
            pltpu.VMEM((length, width), bf16),
            pltpu.VMEM((3, cols, width), bf16),
            pltpu.VMEM((width, width), bf16),
            pltpu.VMEM((2 * width, width), bf16),
            tok_block(f32),
            dma((4 * splits + 6, parts)),
            dma((4 * splits + 6, parts)),
            dma((4 * splits + 6,)),
            dma((2, parts // 2)),
            dma((2, parts // 2)),
            dma((2, parts // 2)),
            dma((2, parts // 2)),
            dma((2, splits)),
            dma((2, splits)),
        ],
        compiler_params=pltpu.CompilerParams(
            collective_id=0, has_side_effects=True, vmem_limit_bytes=60 * 1024 * 1024
        ),
    )(
        tokens,
        cotangent,
        norm_gain,
        w_inner[0],
        w_outer[0],
        cos,
        sin,
        parity,
        spec,
    )
    grad_scale = 1.0 / math.sqrt(length)
    inner = jnp.concatenate([res[2], res[0]], axis=0).T.astype(f32) * grad_scale
    outer = res[1].T.astype(f32) * grad_scale
    return (out[None], grad_in[None], inner[None], outer[None])


def solution(mesh):
    return jax.shard_map(
        on_device,
        mesh=mesh,
        in_specs=(
            P("seq", None),
            P("seq", None),
            P("section", None),
            P("section", None, None),
            P("section", None, None),
            P("section", None),
            P("section", None, None),
            P("section", None, None),
            P("section", None, "seq"),
            P("section", "seq"),
        ),
        out_specs=(
            P("section", "seq", None),
            P("section", "seq", None),
            P("section", "seq", None),
            P("section", "seq", None),
        ),
        check_vma=False,
    )
```
